128 devices in a mesh: stream: 8 (over y, x_hi), span: 16 (over x_lo, z, core).
Axes of the slice: x: 4 (x_hi: 2, x_lo: 2; x = x_hi * 2 + x_lo), y: 4, z: 4, core: 2. Of those that a mesh axis runs over, the one named last changes fastest.
Arguments:
- state: float32 [64, 5, 64, 4, 1024], P('span', None, None, None, 'stream'), as said below
- columns: int32 [16], replicated, may hold values from 1 to 4, 32 in all
- target_profile: float32 [5, 4, 4], replicated, as said below
- fluct_gain: float32 [4, 4], replicated, may hold values from 0.1 to 1.9
Outputs:
- section_state: float32 [64, 5, 64, 4, 1024], P('span', None, None, None, 'stream')
The draws below stay inside these ranges and needn't reach their ends.
Inputs may be any that keep to these rules, and one draw needn't show every extreme that they name: Entry p counts the live columns of span index p, held in its slots 0 to count - 1; the entries sum to 32 and the largest equals 4. `state`: Density, momenta and total energy lie in 0.8 to 1.2, 0.2 to 0.6, -0.3 to 0.3, -0.3 to 0.3 and 2 to 3. `target_profile`: Density, momenta and total energy of the profile lie in 0.9 to 1.1, 0.3 to 0.5, -0.1 to 0.1, -0.1 to 0.1 and 2.4 to 2.6.
All inputs are finite; a program needn't handle non-finite values.
Results may differ from the reference program's by a relative error of at most 0.0003.
Values sent between devices are 32-bit elements; how exact they have to be, the bound alone decides.
No kernel may reach another device: no remote copies, remote signals or barrier semaphores. Data moves between devices by JAX's collectives and lax.ppermute only.
A program may use at most 256 MiB of HBM per device.

```python
import math
import jax
import jax.numpy as jnp
import numpy as np
from jax import lax

NV = 5
NP = 4
NPT = 64
EXD = 128
NEY = 4
ZCAP = 4
NEX = 1024
ZS = 64
N_STREAM = 8
N_SPAN = 16


def draw_state(key, part):
    base = jax.random.uniform(key, (ZS, NV, NPT, NEY, NEX), dtype=jnp.float32)
    lower = jnp.asarray([0.8, 0.2, -0.3, -0.3, 2.0], dtype=jnp.float32).reshape(1, 5, 1, 1, 1)
    upper = jnp.asarray([1.2, 0.6, 0.3, 0.3, 3.0], dtype=jnp.float32).reshape(1, 5, 1, 1, 1)
    return lower + (upper - lower) * base


def draw_target_profile(key, part):
    base = jax.random.uniform(jax.random.fold_in(key, 7), (NV, NP, NEY), dtype=jnp.float32)
    lower = jnp.asarray([0.9, 0.3, -0.1, -0.1, 2.4], dtype=jnp.float32).reshape(5, 1, 1)
    upper = jnp.asarray([1.1, 0.5, 0.1, 0.1, 2.6], dtype=jnp.float32).reshape(5, 1, 1)
    return lower + (upper - lower) * base


def split_up(amount, total, bound, skew):
    weights = [(1 << 20) // math.isqrt(rank ** skew) + 1 for rank in range(2, amount + 1)]
    spare, given = total - bound - (amount - 1), [1] * (amount - 1)
    while spare > 0:
        candidates = [i for i in range(amount - 1) if given[i] < bound]
        whole, remaining = sum([weights[i] for i in candidates]), spare
        for i in candidates:
            addition = min(bound - given[i], max(1, remaining * weights[i] // whole), spare)
            given[i] = given[i] + addition
            spare = spare - addition
    return np.array([bound] + given)


def ragged(own_key, count, total, most, skew):
    if count == 2:
        one = jax.random.randint(own_key, (), max(1, total - most), min(most, total - 1) + 1)
        return jnp.stack([one, total - one])
    tallies = jnp.asarray(split_up(count, total, most, skew), jnp.int32)
    pairs = (count - 1) // 2
    donor, taker = tallies[1:1 + 2 * pairs:2], tallies[2:2 + 2 * pairs:2]
    room = jnp.minimum(donor - 1, most - taker)
    shifted = jax.random.randint(jax.random.fold_in(own_key, 1), (pairs,), 0, 1 << 20) % (room + 1)
    tallies = tallies.at[1:1 + 2 * pairs:2].set(donor - shifted).at[2:2 + 2 * pairs:2].set(taker + shifted)
    return tallies[jax.random.permutation(jax.random.fold_in(own_key, 2), count)]


def setup_inputs(seed: int = 0) -> dict:
    splits = jax.random.split(jax.random.key(seed), 5)
    return {
        "state": draw_state(jax.random.fold_in(splits[4], 71), 0),
        "columns": ragged(splits[1], N_SPAN, ZS // 2, ZCAP, 2).astype(jnp.int32),
        "target_profile": draw_target_profile(jax.random.fold_in(splits[4], 71), 0),
        "fluct_gain": jnp.clip(jax.random.uniform(splits[3], (NP, NEY), jnp.float32, 0.1, 1.9), 0.1, 1.9),
    }


GAMMA = 1.4
VISC = 0.02
COND = VISC * GAMMA / (GAMMA - 1.0) / 0.72
JACOBS = (5.0, 10.0, 5.0)
STEP_DT = 0.004
RELAX = 10.0
WEIGHTS = (1.0 / 6.0, 5.0 / 6.0, 5.0 / 6.0, 1.0 / 6.0)
INV_END = 6.0
MIRROR = (1.0, 1.0, -1.0, 1.0, 1.0)

def derivative_table():
    inner_node = math.sqrt(0.2)
    points = [-1.0, -inner_node, inner_node, 1.0]
    barycentric = []
    for j in range(4):
        product = 1.0
        for k in range(4):
            if k != j:
                product = product * (points[j] - points[k])
        barycentric.append(1.0 / product)
    entries = [[0.0, 0.0, 0.0, 0.0] for i in range(4)]
    for i in range(4):
        diagonal = 0.0
        for j in range(4):
            if i != j:
                entries[i][j] = barycentric[j] / barycentric[i] / (points[i] - points[j])
                diagonal = diagonal - entries[i][j]
        entries[i][i] = diagonal
    return entries

def component(values, index, coordinate_heading):
    return lax.index_in_dim(values, index, coordinate_heading, keepdims=False)

def physical_quantities(state, coordinate_heading):
    density = component(state, 0, coordinate_heading)
    momenta = [component(state, k + 1, coordinate_heading) for k in range(3)]
    energy = component(state, 4, coordinate_heading)
    velocity = [momentum / density for momentum in momenta]
    kinetic = 0.5 * (momenta[0] * velocity[0] + momenta[1] * velocity[1] + momenta[2] * velocity[2])
    pressure = (GAMMA - 1.0) * (energy - kinetic)
    return (state, density, velocity, pressure, energy / density)

def slice_fields(solution_tensors, index, d, keep):
    state = lax.index_in_dim(solution_tensors[0], index, d + 1, keepdims=keep)
    density = lax.index_in_dim(solution_tensors[1], index, d, keepdims=keep)
    velocity = [lax.index_in_dim(entry, index, d, keepdims=keep) for entry in solution_tensors[2]]
    pressure = lax.index_in_dim(solution_tensors[3], index, d, keepdims=keep)
    specific = lax.index_in_dim(solution_tensors[4], index, d, keepdims=keep)
    return (state, density, velocity, pressure, specific)

def pair_flux(left, right, d, coordinate_heading):
    density = 0.5 * (left[1] + right[1])
    velocity = [0.5 * (left[2][k] + right[2][k]) for k in range(3)]
    pressure = 0.5 * (left[3] + right[3])
    specific = 0.5 * (left[4] + right[4])
    carried = density * velocity[d]
    pieces = [carried]
    for k in range(3):
        entry = carried * velocity[k]
        if k == d:
            entry = entry + pressure
        pieces.append(entry)
    pieces.append(carried * specific + pressure * velocity[d])
    return jnp.stack(pieces, axis=coordinate_heading)

def face_flux(left, right, d, coordinate_heading):
    speed_left = jnp.abs(left[2][d]) + jnp.sqrt(GAMMA * left[3] / left[1])
    speed_right = jnp.abs(right[2][d]) + jnp.sqrt(GAMMA * right[3] / right[1])
    speed = jnp.maximum(speed_left, speed_right)
    return pair_flux(left, right, d, coordinate_heading) - 0.5 * jnp.expand_dims(speed, coordinate_heading) * (right[0] - left[0])

def node_column(entries, d, ndim):
    shape = [1] * ndim
    shape[d + 1] = 4
    return jnp.asarray(entries, dtype=jnp.float32).reshape(shape)

def derivative(values, d):
    entries = derivative_table()
    total = None
    for m in range(4):
        factors = node_column([entries[i][m] for i in range(4)], d, values.ndim)
        piece = factors * lax.index_in_dim(values, m, d + 1, keepdims=True)
        total = piece if total is None else total + piece
    return total

def split_volume(solution_tensors, d):
    entries = derivative_table()
    total = None
    for m in range(4):
        partner = slice_fields(solution_tensors, m, d, True)
        flux = pair_flux(solution_tensors, partner, d, 0)
        factors = node_column([2.0 * entries[i][m] for i in range(4)], d, flux.ndim)
        piece = factors * flux
        total = piece if total is None else total + piece
    return total

def place_ends(low, high, d):
    low = jnp.expand_dims(low, d + 1)
    high = jnp.expand_dims(high, d + 1)
    blank = jnp.zeros_like(low)
    return jnp.concatenate([low, blank, blank, high], axis=d + 1)

def outside_faces(face_low, face_high, d, edge_low, edge_high):
    if d == 0:
        bottom_adjoining_solution = jnp.concatenate([edge_low[..., None], face_high[..., :-1]], axis=-1)
        topside_adjoining_solution = jnp.concatenate([face_low[..., 1:], edge_high[..., None]], axis=-1)
    elif d == 1:
        bottom_adjoining_solution = jnp.concatenate([edge_low[..., None, :], face_high[..., :-1, :]], axis=-2)
        topside_adjoining_solution = jnp.concatenate([face_low[..., 1:, :], edge_high[..., None, :]], axis=-2)
    else:
        bottom_adjoining_solution, topside_adjoining_solution = (edge_low, edge_high)
    return (bottom_adjoining_solution, topside_adjoining_solution)

def wall_ghost(face_row):
    signs = jnp.asarray(MIRROR, dtype=jnp.float32).reshape((5,) + (1,) * (face_row.ndim - 1))
    return face_row * signs

def state_edges(face_low, face_high, d, x_low, x_high, z_low, z_high):
    if d == 0:
        return (x_low, x_high)
    if d == 1:
        return (wall_ghost(face_low[..., 0, :]), face_high[..., -1, :])
    return (z_low, z_high)

def thermal_readings(solution_tensors, coordinate_heading):
    return jnp.stack([solution_tensors[2][0], solution_tensors[2][1], solution_tensors[2][2], solution_tensors[3] / solution_tensors[1]], axis=coordinate_heading)

def viscous_flux(solution_tensors, gradients, d, coordinate_heading):
    entry = [component(gradients, n, coordinate_heading) for n in range(12)]
    spread = entry[0] + entry[5] + entry[10]
    stress = []
    for k in range(3):
        value = VISC * (entry[4 * d + k] + entry[4 * k + d])
        if k == d:
            value = value - 2.0 / 3.0 * VISC * spread
        stress.append(value)
    heat = solution_tensors[2][0] * stress[0] + solution_tensors[2][1] * stress[1] + solution_tensors[2][2] * stress[2] + COND * entry[4 * d + 3]
    return jnp.stack(stress + [heat], axis=coordinate_heading)

def column_gradient(column, x_low, x_high, z_low, z_high):
    solution_tensors = physical_quantities(column, 0)
    conservative_solution = thermal_readings(solution_tensors, 0)
    blocks = []
    for d in range(3):
        face_low = lax.index_in_dim(column, 0, d + 1, keepdims=False)
        face_high = lax.index_in_dim(column, 3, d + 1, keepdims=False)
        edge_low, edge_high = state_edges(face_low, face_high, d, x_low, x_high, z_low, z_high)
        bottom_adjoining_solution, topside_adjoining_solution = outside_faces(face_low, face_high, d, edge_low, edge_high)
        bottom_interface_solution = lax.index_in_dim(conservative_solution, 0, d + 1, keepdims=False)
        topside_interface_solution = lax.index_in_dim(conservative_solution, 3, d + 1, keepdims=False)
        bottom_shared_numerical_transport = 0.5 * (bottom_interface_solution + thermal_readings(physical_quantities(bottom_adjoining_solution, 0), 0))
        topside_shared_numerical_transport = 0.5 * (topside_interface_solution + thermal_readings(physical_quantities(topside_adjoining_solution, 0), 0))
        if d == 1:
            wall_row = jnp.concatenate([jnp.zeros_like(bottom_interface_solution[:3, ..., :1, :]), bottom_interface_solution[3:, ..., :1, :]], axis=0)
            bottom_shared_numerical_transport = jnp.concatenate([wall_row, bottom_shared_numerical_transport[..., 1:, :]], axis=-2)
        lifted = derivative(conservative_solution, d) + place_ends(-INV_END * (bottom_shared_numerical_transport - bottom_interface_solution), INV_END * (topside_shared_numerical_transport - topside_interface_solution), d)
        blocks.append(JACOBS[d] * lifted)
    return jnp.concatenate(blocks, axis=0)

def column_update(column, gradients, x_low, x_high, z_low, z_high, xv_low, xv_high, zv_low, zv_high):
    solution_tensors = physical_quantities(column, 0)
    rate = None
    for d in range(3):
        face_low = lax.index_in_dim(column, 0, d + 1, keepdims=False)
        face_high = lax.index_in_dim(column, 3, d + 1, keepdims=False)
        edge_low, edge_high = state_edges(face_low, face_high, d, x_low, x_high, z_low, z_high)
        bottom_adjoining_solution, topside_adjoining_solution = outside_faces(face_low, face_high, d, edge_low, edge_high)
        inner_low = slice_fields(solution_tensors, 0, d, False)
        inner_high = slice_fields(solution_tensors, 3, d, False)
        flux_low = face_flux(physical_quantities(bottom_adjoining_solution, 0), inner_low, d, 0) - pair_flux(inner_low, inner_low, d, 0)
        flux_high = face_flux(inner_high, physical_quantities(topside_adjoining_solution, 0), d, 0) - pair_flux(inner_high, inner_high, d, 0)
        inviscid = split_volume(solution_tensors, d) + place_ends(-INV_END * flux_low, INV_END * flux_high, d)
        viscous_all = viscous_flux(solution_tensors, gradients, d, 0)
        fv_low = lax.index_in_dim(viscous_all, 0, d + 1, keepdims=False)
        fv_high = lax.index_in_dim(viscous_all, 3, d + 1, keepdims=False)
        if d == 0:
            vedge_low, vedge_high = (xv_low, xv_high)
        elif d == 1:
            vedge_low, vedge_high = (fv_low[..., 0, :], fv_high[..., -1, :])
        else:
            vedge_low, vedge_high = (zv_low, zv_high)
        vbelow, vabove = outside_faces(fv_low, fv_high, d, vedge_low, vedge_high)
        vstar_low = 0.5 * (fv_low + vbelow)
        vstar_high = 0.5 * (fv_high + vabove)
        viscous = derivative(viscous_all, d) + place_ends(-INV_END * (vstar_low - fv_low), INV_END * (vstar_high - fv_high), d)
        viscous = jnp.concatenate([jnp.zeros_like(viscous[:1]), viscous], axis=0)
        piece = JACOBS[d] * (viscous - inviscid)
        rate = piece if rate is None else rate + piece
    return column + STEP_DT * rate

def reference(state, columns, target_profile, fluct_gain):
    slots = state.shape[0]
    layers = state.shape[3]
    length = state.shape[4]
    element_view = state.reshape(slots, 5, 4, 4, 4, layers, length)
    counts = columns.astype(jnp.int32)
    starts = (jnp.cumsum(counts).astype(jnp.int32) - counts).astype(jnp.int32)
    slot_ids = jnp.arange(slots, dtype=jnp.int32)
    owner = (slot_ids // ZCAP).astype(jnp.int32)
    within = (slot_ids % ZCAP).astype(jnp.int32)
    alive = within < counts[owner]
    rank = (starts[owner] + within).astype(jnp.int32)
    total = ZS // 2

    def slot_of(rank_value):
        holder = (lax.optimization_barrier(jnp.sum((starts[None, :] <= rank_value[:, None]).astype(jnp.int32), axis=1)) - 1).astype(jnp.int32)
        return (holder * ZCAP + rank_value - starts[holder]).astype(jnp.int32)
    left_slot = jnp.where(alive, slot_of((rank - 1 + total) % total), slot_ids)
    right_slot = jnp.where(alive, slot_of((rank + 1) % total), slot_ids)
    node_weights = jnp.asarray(WEIGHTS, dtype=jnp.float32).reshape(1, 1, 1, 4, 1, 1)
    stations = element_view[:, :, 0, :, :, :, ::EXD]
    weighted = jnp.where(alive[:, None, None, None, None, None], stations * node_weights, 0.0)
    profiles = lax.optimization_barrier(jnp.sum(weighted, axis=(0, 3))) / float(ZS)
    own_recycled = target_profile[None, :, :, None, :, None] + fluct_gain[None, None, :, None, :, None] * (stations - profiles[None, :, :, None, :, :])
    recycled = jnp.roll(own_recycled, -(N_STREAM // 2), axis=5)
    inflow = recycled[..., 0]

    def gradients_of(slot):
        column = element_view[slot]
        z_low = element_view[left_slot[slot]][:, :, :, 3]
        z_high = element_view[right_slot[slot]][:, :, :, 0]
        x_high = column[:, 3, :, :, :, -1]
        return (column, x_high, column_gradient(column, inflow[slot], x_high, z_low, z_high))

    def faces_of(slot):
        column, x_high, gradients = gradients_of(slot)
        viscous_z = viscous_flux(physical_quantities(column, 0), gradients, 2, 0)
        return jnp.stack([viscous_z[:, :, :, 0], viscous_z[:, :, :, 3]])
    span_fluxes = lax.map(faces_of, slot_ids)

    def update_of(slot):
        column, x_high, gradients = gradients_of(slot)
        z_low = element_view[left_slot[slot]][:, :, :, 3]
        z_high = element_view[right_slot[slot]][:, :, :, 0]
        xv_low = viscous_flux(physical_quantities(inflow[slot], 0), gradients[:, 0, :, :, :, 0], 0, 0)
        xv_high = viscous_flux(physical_quantities(x_high, 0), gradients[:, 3, :, :, :, -1], 0, 0)
        zv_low = span_fluxes[left_slot[slot], 1]
        zv_high = span_fluxes[right_slot[slot], 0]
        updated = column_update(column, gradients, inflow[slot], x_high, z_low, z_high, xv_low, xv_high, zv_low, zv_high)
        return jnp.where(alive[slot], updated, column)
    result = lax.map(update_of, slot_ids)
    relaxation = jnp.where(alive[:, None, None, None, None, None], STEP_DT * RELAX * (recycled - stations), 0.0)
    result = result.at[:, :, 0, :, :, :, ::EXD].add(relaxation)
    return result.reshape(state.shape)
```

```python
import functools
import math

import jax
import jax.numpy as jnp
from jax import lax
from jax.experimental import pallas as pl
from jax.experimental.pallas import tpu as pltpu
from jax.sharding import PartitionSpec as P

GAMMA = 1.4
VISC = 0.02
COND = VISC * GAMMA / (GAMMA - 1.0) / 0.72
JACOBS = (5.0, 10.0, 5.0)
STEP_DT = 0.004
RELAX = 10.0
HR, HV, HP, HE, TT, HC = 0, 1, 4, 5, 6, 7
NPRIM = 8
F32 = jnp.float32


def derivative_table():
    inner_node = math.sqrt(0.2)
    points = [-1.0, -inner_node, inner_node, 1.0]
    barycentric = []
    for j in range(4):
        product = 1.0
        for k in range(4):
            if k != j:
                product = product * (points[j] - points[k])
        barycentric.append(1.0 / product)
    entries = [[0.0] * 4 for _ in range(4)]
    for i in range(4):
        diagonal = 0.0
        for j in range(4):
            if i != j:
                entries[i][j] = barycentric[j] / barycentric[i] / (points[i] - points[j])
                diagonal = diagonal - entries[i][j]
        entries[i][i] = diagonal
    return entries


D = derivative_table()
Q = [[(1.0 / 6.0, 5.0 / 6.0, 5.0 / 6.0, 1.0 / 6.0)[i] * D[i][j] for j in range(4)] for i in range(4)]


def lane_iota():
    return lax.broadcasted_iota(jnp.int32, (8, 128), 1)


def sub_iota():
    return lax.broadcasted_iota(jnp.int32, (8, 128), 0)


def swap(x):
    return pltpu.roll(x, 4, 0)


def lane_of(node):
    b, c = node // 4, node % 4
    return 8 * (c % 2) + 2 * b + c // 2


def bases(d, i):
    if d == 0:
        return i, 16
    if d == 1:
        return 16 * (i // 4) + i % 4, 4
    return 4 * i, 1


def to_prims(u):
    inv = 1.0 / u[0]
    hv = [(0.5 * u[k + 1]) * inv for k in range(3)]
    kin = u[1] * hv[0] + u[2] * hv[1] + u[3] * hv[2]
    hp = (0.5 * (GAMMA - 1.0)) * (u[4] - kin)
    he = (0.5 * u[4]) * inv
    temp = (2.0 * hp) * inv
    hc = 0.5 * jnp.sqrt(GAMMA * temp)
    return [0.5 * u[0], *hv, hp, he, temp, hc]


def pair_terms(left, right, d, scale):
    kr = scale * (left[HR] + right[HR])
    vel = [left[HV + k] + right[HV + k] for k in range(3)]
    kp = scale * (left[HP] + right[HP])
    he = left[HE] + right[HE]
    carried = kr * vel[d]
    out = [carried]
    for k in range(3):
        entry = carried * vel[k]
        if k == d:
            entry = entry + kp
        out.append(entry)
    out.append(carried * he + kp * vel[d])
    return out


def face_terms(left, right, d, scale):
    flux = pair_terms(left, right, d, scale)
    speed = jnp.maximum(jnp.abs(left[HV + d]) + left[HC], jnp.abs(right[HV + d]) + right[HC])
    two = (2.0 * scale) * speed
    four = two + two
    out = [flux[0] - two * (right[HR] - left[HR])]
    for k in range(3):
        out.append(flux[k + 1] - four * (right[HR] * right[HV + k] - left[HR] * left[HV + k]))
    out.append(flux[4] - four * (right[HR] * right[HE] - left[HR] * left[HE]))
    return out


def line_inviscid(nodes, low, high, d):
    scale = 2.4 * JACOBS[d] * STEP_DT
    g = {}
    for i in range(4):
        for j in range(i + 1, 4):
            g[i, j] = pair_terms(nodes[i], nodes[j], d, scale * Q[i][j])
    f_low = face_terms(low, nodes[0], d, 0.5 * scale)
    f_high = face_terms(nodes[3], high, d, 0.5 * scale)
    r0 = [5.0 * (f_low[v] - g[0, 1][v] - g[0, 2][v] - g[0, 3][v]) for v in range(5)]
    r1 = [g[0, 1][v] - g[1, 2][v] - g[1, 3][v] for v in range(5)]
    r2 = [g[0, 2][v] + g[1, 2][v] - g[2, 3][v] for v in range(5)]
    r3 = [5.0 * (g[0, 3][v] + g[1, 3][v] + g[2, 3][v] - f_high[v]) for v in range(5)]
    return r0, r1, r2, r3


def line_derivative(w, low, high, scale):
    c = [[scale * D[i][j] for j in range(4)] for i in range(4)]
    three = 3.0 * scale
    return (
        c[0][1] * w[1] + c[0][2] * w[2] + c[0][3] * w[3] - three * low,
        c[1][0] * w[0] + c[1][2] * w[2] + c[1][3] * w[3],
        c[2][0] * w[0] + c[2][1] * w[1] + c[2][3] * w[3],
        c[3][0] * w[0] + c[3][1] * w[1] + c[3][2] * w[2] + three * high,
    )


def packed(value, at_lane, lane):
    return pltpu.roll(value, lax.rem(at_lane + 128 - lane, 128), 1)


def pack_kernel(meta, st, xl, xh, zl, zh):
    n = meta[0]
    lanes = lane_iota()
    low_half = sub_iota() < 4
    for side, (out, a, src) in enumerate(((xl, 0, 0), (xh, 3, 127))):

        def per_field(v, carry, out=out, a=a, src=src):
            gathered = []
            for s in range(4):
                acc = jnp.zeros((8, 128), F32)
                for k in range(8):
                    moved = pltpu.roll(st[s, v, 8 * a + k], (k + 128 - src) % 128, 1)
                    acc = jnp.where(lanes == k, moved, acc)
                gathered.append(acc)
            for q in range(2):
                za, zb = gathered[2 * q], gathered[2 * q + 1]
                even = jnp.where(low_half, za, swap(zb))
                odd = jnp.where(low_half, swap(za), zb)
                out[q, v] = jnp.where(lanes < 8, even, pltpu.roll(odd, 8, 1))
            return carry

        lax.fori_loop(0, 5, per_field, 0)

    def z_field(v, carry):
        for m in range(8):
            zl[v, m] = jnp.where(low_half, st[0, v, 2 * m], swap(st[0, v, 2 * (m + 8)]))
            zh[v, m] = jnp.where(
                low_half, swap(st[n - 1, v, 2 * m + 1]), st[n - 1, v, 2 * (m + 8) + 1]
            )
        return carry

    lax.fori_loop(0, 5, z_field, 0)


def small_table(get, lanes, subs):
    b_of = lax.rem(lanes, 8) // 2
    y_of = lax.rem(subs, 4)
    acc = jnp.zeros((8, 128), F32)
    for b in range(4):
        for y in range(4):
            acc = jnp.where((b_of == b) & (y_of == y), get(b, y), acc)
    return acc


def recycled_planes(plane, sums, target, gain, write):
    lanes, subs = lane_iota(), sub_iota()
    even = lax.rem(lanes, 2) == 0
    gains = small_table(lambda b, y: gain[4 * b + y], lanes, subs)
    for v in range(5):
        t = sums[v]
        t = t + swap(t)
        t = t + pltpu.roll(t, 120, 1)
        t = t + pltpu.roll(t, 127, 1)
        t = jnp.where(even, t, pltpu.roll(t, 1, 1))
        profile = jnp.where(lanes < 8, t, pltpu.roll(t, 8, 1))
        wanted = small_table(lambda b, y, v=v: target[16 * v + 4 * b + y], lanes, subs)
        for q in range(2):
            write(q, v, wanted + gains * (plane[q, v] - profile))


def flux_kernel(
    meta, target, gain, st, xfl, xfr, xown, zfl, zfr, plane, sums,
    rate, gflux, gxl, gxh, gzl, gzh, rec, prim, xg, zg, grad,
):
    n, inlet, outlet = meta[0], meta[1], meta[2]
    pairs = (n + 1) // 2
    lanes, subs = lane_iota(), sub_iota()
    low_half = subs < 4
    y_of = lax.rem(subs, 4)
    half = subs // 4

    def write_rec(q, v, value):
        rec[q, v] = value

    recycled_planes(plane, sums, target, gain, write_rec)

    for q in range(2):
        lo = [jnp.where(inlet == 1, rec[q, v], xfl[q, v]) for v in range(5)]
        hi = [jnp.where(outlet == 1, xown[q, v], xfr[q, v]) for v in range(5)]
        used = lanes < 16
        for side, u in enumerate((lo, hi)):
            u = [jnp.where(used, x, 1.0) for x in u]
            for f, x in enumerate(to_prims(u)):
                xg[side, q, f] = x

    def z_ghost(m, carry):
        for side, src in enumerate((zfl, zfr)):
            for f, x in enumerate(to_prims([src[v, m] for v in range(5)])):
                other = swap(x)
                zg[side, f, m] = jnp.where(low_half, x, other)
                zg[side, f, m + 8] = jnp.where(low_half, other, x)
        return carry

    lax.fori_loop(0, 8, z_ghost, 0)

    def prims_of(q, carry):
        def nodes(kk, inner):
            first, second = [], []
            for v in range(5):
                a, b = st[2 * q, v, kk], st[2 * q + 1, v, kk]
                first.append(jnp.where(low_half, a, swap(b)))
                second.append(jnp.where(low_half, swap(a), b))
            for f, x in enumerate(to_prims(first)):
                prim[q, f, 2 * kk] = x
            for f, x in enumerate(to_prims(second)):
                prim[q, f, 2 * kk + 1] = x
            return inner

        return lax.fori_loop(0, 32, nodes, carry)

    lax.fori_loop(0, pairs, prims_of, 0)

    def direction(d):
        def per_pair(q, carry):
            slot = 2 * q + half
            before, after = jnp.maximum(q - 1, 0), jnp.minimum(q + 1, 1)

            def line(i, inner):
                base, stride = bases(d, i)
                at = [base + j * stride for j in range(4)]
                nodes = [[prim[q, f, at[j]] for f in range(NPRIM)] for j in range(4)]
                low, high = [], []
                if d == 0:
                    lane = lane_of(i)
                    for f in range(NPRIM):
                        ghost = packed(xg[0, q, f], 0, lane)
                        low.append(jnp.where(lanes == 0, ghost, pltpu.roll(nodes[3][f], 1, 1)))
                        ghost = packed(xg[1, q, f], 127, lane)
                        high.append(
                            jnp.where(lanes == 127, ghost, pltpu.roll(nodes[0][f], 127, 1))
                        )
                elif d == 1:
                    for f in range(NPRIM):
                        wall = -nodes[0][f] if f == HV + 1 else nodes[0][f]
                        low.append(jnp.where(y_of == 0, wall, pltpu.roll(nodes[3][f], 1, 0)))
                        high.append(
                            jnp.where(y_of == 3, nodes[3][f], pltpu.roll(nodes[0][f], 7, 0))
                        )
                else:
                    for f in range(NPRIM):
                        prev, nxt = prim[before, f, at[3]], prim[after, f, at[0]]
                        x = swap(jnp.where(low_half, nodes[3][f], prev))
                        low.append(jnp.where(slot == 0, zg[0, f, i], x))
                        x = swap(jnp.where(low_half, nxt, nodes[0][f]))
                        high.append(jnp.where(slot == n - 1, zg[1, f, i], x))
                change = line_inviscid(nodes, low, high, d)
                for j in range(4):
                    for v in range(5):
                        if d == 0:
                            rate[q, v, at[j]] = change[j][v]
                        else:
                            rate[q, v, at[j]] = rate[q, v, at[j]] + change[j][v]
                for k in range(4):
                    f = HV + k if k < 3 else TT
                    scale = JACOBS[d] * (2.0 * VISC if k < 3 else COND)
                    w_low = low[f]
                    if d == 1 and k == 1:
                        pass
                    elif d == 1 and k < 3:
                        w_low = jnp.where(y_of == 0, -nodes[0][f], w_low)
                    lifted = line_derivative([nodes[j][f] for j in range(4)], w_low, high[f], scale)
                    for j in range(4):
                        grad[q, 4 * d + k, at[j]] = lifted[j]
                return inner

            return lax.fori_loop(0, 16, line, carry)

        lax.fori_loop(0, pairs, per_pair, 0)

    for d in range(3):
        direction(d)

    def fluxes(q, carry):
        def node(m, inner):
            e = [grad[q, k, m] for k in range(12)]
            hv = [prim[q, HV + k, m] for k in range(3)]
            spread = (2.0 / 3.0) * (e[0] + e[5] + e[10])
            t = {}
            for i in range(3):
                t[i, i] = (e[5 * i] + e[5 * i]) - spread
                for j in range(i + 1, 3):
                    t[i, j] = t[j, i] = e[4 * i + j] + e[4 * j + i]
            for index, key in enumerate(((0, 0), (0, 1), (0, 2), (1, 1), (1, 2), (2, 2))):
                gflux[q, index, m] = t[key]
            for i in range(3):
                h = hv[0] * t[i, 0] + hv[1] * t[i, 1] + hv[2] * t[i, 2]
                gflux[q, 6 + i, m] = (h + h) + e[4 * i + 3]
            return inner

        return lax.fori_loop(0, 64, node, carry)

    lax.fori_loop(0, pairs, fluxes, 0)

    for q in range(2):
        for f in range(4):
            gxl[q, f] = jnp.zeros((8, 128), F32)
            gxh[q, f] = jnp.zeros((8, 128), F32)

    def x_faces(q, carry):
        def node(i, inner):
            lane = lane_of(i)
            for f, src in enumerate((0, 1, 2, 6)):
                lo = pltpu.roll(gflux[q, src, i], lane, 1)
                hi = pltpu.roll(gflux[q, src, 48 + i], lax.rem(lane + 1, 128), 1)
                gxl[q, f] = jnp.where(lanes == lane, lo, gxl[q, f])
                gxh[q, f] = jnp.where(lanes == lane, hi, gxh[q, f])
            return inner

        return lax.fori_loop(0, 16, node, carry)

    lax.fori_loop(0, pairs, x_faces, 0)
    last_q, last_half = (n - 1) // 2, lax.rem(n - 1, 2)

    def z_faces(m, carry):
        for f, src in enumerate((2, 4, 5, 8)):
            gzl[f, m] = jnp.where(low_half, gflux[0, src, 4 * m], swap(gflux[0, src, 4 * (m + 8)]))
            x, y = gflux[last_q, src, 4 * m + 3], gflux[last_q, src, 4 * (m + 8) + 3]
            even = jnp.where(low_half, x, swap(y))
            odd = jnp.where(low_half, swap(x), y)
            gzh[f, m] = jnp.where(last_half == 0, even, odd)
        return carry

    lax.fori_loop(0, 8, z_faces, 0)


GFIELDS = ((0, 1, 2, 6), (1, 3, 4, 7), (2, 4, 5, 8))


def update_kernel(
    meta, st, rate_in, gflux, xown, xfl, xfr, gxfl, gxfr, gzfl, gzfr, rec, out, rate, zg
):
    n, inlet, outlet = meta[0], meta[1], meta[2]
    pairs = (n + 1) // 2
    lanes, subs = lane_iota(), sub_iota()
    low_half = subs < 4
    y_of = lax.rem(subs, 4)
    half = subs // 4

    def z_ghost(m, carry):
        for side, src in enumerate((gzfl, gzfr)):
            for f in range(4):
                x = src[f, m]
                other = swap(x)
                zg[side, f, m] = jnp.where(low_half, x, other)
                zg[side, f, m + 8] = jnp.where(low_half, other, x)
        return carry

    lax.fori_loop(0, 8, z_ghost, 0)

    def direction(d):
        def per_pair(q, carry):
            slot = 2 * q + half
            before, after = jnp.maximum(q - 1, 0), jnp.minimum(q + 1, 1)
            if d == 0:
                dv = [
                    rec[q, k + 1] / rec[q, 0] - xown[q, k + 1] / xown[q, 0] for k in range(3)
                ]

            def line(i, inner):
                base, stride = bases(d, i)
                at = [base + j * stride for j in range(4)]
                g = [[gflux[q, f, at[j]] for f in GFIELDS[d]] for j in range(4)]
                low, high = [], []
                if d == 0:
                    lane = lane_of(i)
                    inner_low = list(g[0])
                    for k in range(3):
                        inner_low[3] = inner_low[3] + packed(dv[k], 0, lane) * g[0][k]
                    for f in range(4):
                        ghost = packed(gxfl[q, f], 0, lane)
                        ghost = jnp.where(inlet == 1, inner_low[f], ghost)
                        low.append(jnp.where(lanes == 0, ghost, pltpu.roll(g[3][f], 1, 1)))
                        ghost = packed(gxfr[q, f], 127, lane)
                        ghost = jnp.where(outlet == 1, g[3][f], ghost)
                        high.append(jnp.where(lanes == 127, ghost, pltpu.roll(g[0][f], 127, 1)))
                elif d == 1:
                    for f in range(4):
                        low.append(jnp.where(y_of == 0, g[0][f], pltpu.roll(g[3][f], 1, 0)))
                        high.append(jnp.where(y_of == 3, g[3][f], pltpu.roll(g[0][f], 7, 0)))
                else:
                    for f in range(4):
                        src = GFIELDS[d][f]
                        prev, nxt = gflux[before, src, at[3]], gflux[after, src, at[0]]
                        x = swap(jnp.where(low_half, g[3][f], prev))
                        low.append(jnp.where(slot == 0, zg[0, f, i], x))
                        x = swap(jnp.where(low_half, nxt, g[0][f]))
                        high.append(jnp.where(slot == n - 1, zg[1, f, i], x))
                for f in range(4):
                    change = line_derivative(
                        [g[j][f] for j in range(4)], low[f], high[f], JACOBS[d] * STEP_DT
                    )
                    for j in range(4):
                        if d == 0:
                            rate[q, f, at[j]] = rate_in[q, f + 1, at[j]] + change[j]
                        else:
                            rate[q, f, at[j]] = rate[q, f, at[j]] + change[j]
                if d == 2:
                    pass
                return inner

            return lax.fori_loop(0, 16, line, carry)

        lax.fori_loop(0, pairs, per_pair, 0)

    for d in range(3):
        direction(d)

    for q in range(2):
        live_a = jnp.where(2 * q < n, 1.0, 0.0)
        live_b = jnp.where(2 * q + 1 < n, 1.0, 0.0)

        @pl.when(2 * q < n)
        def _(q=q):
            def nodes(kk, carry):
                for v in range(5):
                    if v == 0:
                        x, y = rate_in[q, 0, 2 * kk], rate_in[q, 0, 2 * kk + 1]
                    else:
                        x, y = rate[q, v - 1, 2 * kk], rate[q, v - 1, 2 * kk + 1]
                    out[2 * q, v, kk] = st[2 * q, v, kk] + jnp.where(low_half, x, swap(y))
                    b = st[2 * q + 1, v, kk]
                    z = b + jnp.where(low_half, swap(x), y)
                    out[2 * q + 1, v, kk] = jnp.where(2 * q + 1 < n, z, b)
                return carry

            lax.fori_loop(0, 32, nodes, 0)

            def relax(k, carry):
                lane = 2 * (k // 2) + lax.rem(k, 2)
                for v in range(5):
                    step = (STEP_DT * RELAX) * (rec[q, v] - xown[q, v])
                    x = packed(step, 0, lane)
                    y = packed(step, 0, lane + 8)
                    a = jnp.where(low_half, x, swap(y))
                    b = jnp.where(low_half, swap(x), y)
                    out[2 * q, v, k] = out[2 * q, v, k] + jnp.where(lanes == 0, a, 0.0)
                    keep = (lanes == 0) & (2 * q + 1 < n)
                    out[2 * q + 1, v, k] = out[2 * q + 1, v, k] + jnp.where(keep, b, 0.0)
                return carry

            lax.fori_loop(0, 8, relax, 0)

        @pl.when(2 * q >= n)
        def _(q=q):
            out[2 * q] = st[2 * q]
            out[2 * q + 1] = st[2 * q + 1]


def shape(*dims):
    return jax.ShapeDtypeStruct(dims, F32)


def vspec():
    return pl.BlockSpec(memory_space=pltpu.VMEM)


def sspec():
    return pl.BlockSpec(memory_space=pltpu.SMEM)


PARAMS = pltpu.CompilerParams(vmem_limit_bytes=56 << 20)


def shifted(array, axis, by):
    count = lax.axis_size(axis)
    return lax.ppermute(array, axis, [(i, (i + by) % count) for i in range(count)])


def on_device(state, columns, target_profile, fluct_gain):
    st = state.reshape(4, 5, 32, 8, 128)
    streams, spans = lax.axis_size("stream"), lax.axis_size("span")
    stream_index = lax.axis_index("stream")
    n = lax.dynamic_index_in_dim(columns, lax.axis_index("span"), 0, keepdims=False)
    meta = jnp.stack(
        [
            n,
            (stream_index == 0).astype(jnp.int32),
            (stream_index == streams - 1).astype(jnp.int32),
        ]
    )
    xl, xh, zl, zh = pl.pallas_call(
        pack_kernel,
        out_shape=(shape(2, 5, 8, 128), shape(2, 5, 8, 128), shape(5, 8, 8, 128), shape(5, 8, 8, 128)),
        in_specs=[sspec(), vspec()],
        out_specs=(vspec(),) * 4,
        compiler_params=PARAMS,
        name="pack",
    )(meta, st)
    plane = shifted(xl, "stream", streams // 2)
    zfl = shifted(zh, "span", 1)
    zfr = shifted(zl, "span", -1)
    xfl = shifted(xh, "stream", 1)
    xfr = shifted(xl, "stream", -1)
    lanes = lax.broadcasted_iota(jnp.int32, (2, 1, 8, 128), 3)
    slots = 2 * lax.broadcasted_iota(jnp.int32, (2, 1, 8, 128), 0) + (
        lax.broadcasted_iota(jnp.int32, (2, 1, 8, 128), 2) // 4
    )
    c_of = 2 * (lanes % 2) + lanes // 8
    weight = jnp.where((c_of == 0) | (c_of == 3), 1.0 / 6.0, 5.0 / 6.0) / float(4 * spans)
    weight = jnp.where((lanes < 16) & (slots < n), weight, 0.0)
    sums = jnp.sum(plane * weight, axis=0)
    step = 1
    while step < spans:
        sums = sums + shifted(sums, "span", step)
        step *= 2
    target, gain = target_profile.reshape(-1), fluct_gain.reshape(-1)
    rate, gflux, gxl, gxh, gzl, gzh, rec = pl.pallas_call(
        flux_kernel,
        out_shape=(
            shape(2, 5, 64, 8, 128),
            shape(2, 9, 64, 8, 128),
            shape(2, 4, 8, 128),
            shape(2, 4, 8, 128),
            shape(4, 8, 8, 128),
            shape(4, 8, 8, 128),
            shape(2, 5, 8, 128),
        ),
        in_specs=[sspec()] * 3 + [vspec()] * 8,
        out_specs=(vspec(),) * 7,
        scratch_shapes=[
            pltpu.VMEM((2, NPRIM, 64, 8, 128), F32),
            pltpu.VMEM((2, 2, NPRIM, 8, 128), F32),
            pltpu.VMEM((2, NPRIM, 16, 8, 128), F32),
            pltpu.VMEM((2, 12, 64, 8, 128), F32),
        ],
        compiler_params=PARAMS,
        name="fluxes",
    )(meta, target, gain, st, xfl, xfr, xh, zfl, zfr, plane, sums)
    gxfl = shifted(gxh, "stream", 1)
    gxfr = shifted(gxl, "stream", -1)
    gzfl = shifted(gzh, "span", 1)
    gzfr = shifted(gzl, "span", -1)
    out = pl.pallas_call(
        update_kernel,
        out_shape=shape(4, 5, 32, 8, 128),
        in_specs=[sspec()] + [vspec()] * 11,
        out_specs=vspec(),
        scratch_shapes=[
            pltpu.VMEM((2, 4, 64, 8, 128), F32),
            pltpu.VMEM((2, 4, 16, 8, 128), F32),
        ],
        compiler_params=PARAMS,
        name="update",
    )(meta, st, rate, gflux, xl, xfl, xfr, gxfl, gxfr, gzfl, gzfr, rec)
    return out.reshape(state.shape)


def solution(mesh):
    placed = (P("span", None, None, None, "stream"), P(), P(), P())
    return jax.shard_map(
        on_device,
        mesh=mesh,
        in_specs=placed,
        out_specs=P("span", None, None, None, "stream"),
        check_vma=False,
    )
```

```python
import functools
import math

import jax
import jax.numpy as jnp
from jax import lax
from jax.experimental import pallas as pl
from jax.experimental.pallas import tpu as pltpu
from jax.sharding import PartitionSpec as P

GAMMA = 1.4
VISC = 0.02
COND = VISC * GAMMA / (GAMMA - 1.0) / 0.72
JACOBS = (5.0, 10.0, 5.0)
STEP_DT = 0.004
RELAX = 10.0
HR, HV, HP, HE, TT, HC = 0, 1, 4, 5, 6, 7
NPRIM = 8
F32 = jnp.float32


def derivative_table():
    inner_node = math.sqrt(0.2)
    points = [-1.0, -inner_node, inner_node, 1.0]
    barycentric = []
    for j in range(4):
        product = 1.0
        for k in range(4):
            if k != j:
                product = product * (points[j] - points[k])
        barycentric.append(1.0 / product)
    entries = [[0.0] * 4 for _ in range(4)]
    for i in range(4):
        diagonal = 0.0
        for j in range(4):
            if i != j:
                entries[i][j] = barycentric[j] / barycentric[i] / (points[i] - points[j])
                diagonal = diagonal - entries[i][j]
        entries[i][i] = diagonal
    return entries


D = derivative_table()
Q = [[(1.0 / 6.0, 5.0 / 6.0, 5.0 / 6.0, 1.0 / 6.0)[i] * D[i][j] for j in range(4)] for i in range(4)]


def lane_iota():
    return lax.broadcasted_iota(jnp.int32, (8, 128), 1)


def sub_iota():
    return lax.broadcasted_iota(jnp.int32, (8, 128), 0)


def swap(x):
    return pltpu.roll(x, 4, 0)


def lane_of(node):
    return 8 * (node % 4) + 2 * (node // 4)


def bases(d, i):
    if d == 0:
        return i, 16
    if d == 1:
        return 16 * (i // 4) + i % 4, 4
    return 4 * i, 1


def to_prims(u):
    inv = 1.0 / u[0]
    hv = [(0.5 * u[k + 1]) * inv for k in range(3)]
    kin = u[1] * hv[0] + u[2] * hv[1] + u[3] * hv[2]
    hp = (0.5 * (GAMMA - 1.0)) * (u[4] - kin)
    he = (0.5 * u[4]) * inv
    temp = (2.0 * hp) * inv
    hc = 0.5 * jnp.sqrt(GAMMA * temp)
    return [0.5 * u[0], *hv, hp, he, temp, hc]


def pair_terms(left, right, d, scale):
    kr = scale * (left[HR] + right[HR])
    vel = [left[HV + k] + right[HV + k] for k in range(3)]
    kp = scale * (left[HP] + right[HP])
    he = left[HE] + right[HE]
    carried = kr * vel[d]
    out = [carried]
    for k in range(3):
        entry = carried * vel[k]
        if k == d:
            entry = entry + kp
        out.append(entry)
    out.append(carried * he + kp * vel[d])
    return out


def face_terms(left, right, d, scale):
    flux = pair_terms(left, right, d, scale)
    speed = jnp.maximum(jnp.abs(left[HV + d]) + left[HC], jnp.abs(right[HV + d]) + right[HC])
    two = (2.0 * scale) * speed
    four = two + two
    out = [flux[0] - two * (right[HR] - left[HR])]
    for k in range(3):
        out.append(flux[k + 1] - four * (right[HR] * right[HV + k] - left[HR] * left[HV + k]))
    out.append(flux[4] - four * (right[HR] * right[HE] - left[HR] * left[HE]))
    return out


def line_inviscid(nodes, low, high, d):
    scale = 2.4 * JACOBS[d] * STEP_DT
    g = {}
    for i in range(4):
        for j in range(i + 1, 4):
            g[i, j] = pair_terms(nodes[i], nodes[j], d, scale * Q[i][j])
    f_low = face_terms(low, nodes[0], d, 0.5 * scale)
    f_high = face_terms(nodes[3], high, d, 0.5 * scale)
    r0 = [5.0 * (f_low[v] - g[0, 1][v] - g[0, 2][v] - g[0, 3][v]) for v in range(5)]
    r1 = [g[0, 1][v] - g[1, 2][v] - g[1, 3][v] for v in range(5)]
    r2 = [g[0, 2][v] + g[1, 2][v] - g[2, 3][v] for v in range(5)]
    r3 = [5.0 * (g[0, 3][v] + g[1, 3][v] + g[2, 3][v] - f_high[v]) for v in range(5)]
    return r0, r1, r2, r3


def line_derivative(w, low, high, scale):
    c = [[scale * D[i][j] for j in range(4)] for i in range(4)]
    three = 3.0 * scale
    return (
        c[0][1] * w[1] + c[0][2] * w[2] + c[0][3] * w[3] - three * low,
        c[1][0] * w[0] + c[1][2] * w[2] + c[1][3] * w[3],
        c[2][0] * w[0] + c[2][1] * w[1] + c[2][3] * w[3],
        c[3][0] * w[0] + c[3][1] * w[1] + c[3][2] * w[2] + three * high,
    )


def packed(value, at_lane, lane):
    return pltpu.roll(value, lax.rem(at_lane + 128 - lane, 128), 1)


def masks():
    lanes, subs = lane_iota(), sub_iota()
    return lanes, subs, subs < 4, lax.rem(lanes, 2) == 0


def place(axes_ref):
    n = axes_ref[2]
    return n, axes_ref[0] == 0, axes_ref[0] == axes_ref[1] - 1


W_SCALE = (2.0 * VISC, 2.0 * VISC, 2.0 * VISC, COND)


def readings(prims):
    return [prims[HV], prims[HV + 1], prims[HV + 2], prims[TT]]


def pack_kernel(st, faces, planes):
    lanes, subs, low_half, high_end = masks()
    even_c = lax.rem(lanes // 8, 2) == 0

    def per_field(v, carry):
        for a in range(4):
            gathered = []
            for s in range(4):
                acc = jnp.ones((8, 128), F32)
                for k in range(8):
                    target = 16 * (k % 2) + 2 * (k // 2)
                    moved = pltpu.roll(st[s, v, 8 * a + k], target + 1, 1)
                    acc = jnp.where(lanes // 2 == target // 2, moved, acc)
                gathered.append(acc)
            for q in range(2):
                za, zb = gathered[2 * q], gathered[2 * q + 1]
                even = jnp.where(low_half, za, swap(zb))
                odd = jnp.where(low_half, swap(za), zb)
                planes[q, a, v] = jnp.where(even_c, even, pltpu.roll(odd, 8, 1))
        return carry

    lax.fori_loop(0, 5, per_field, 0)
    for q in range(2):
        w = []
        for a in range(4):
            w.append(readings(to_prims([planes[q, a, v] for v in range(5)])))
        for v in range(5):
            faces[q, v] = jnp.where(high_end, planes[q, 3, v], planes[q, 0, v])
        for f in range(4):
            scale = JACOBS[0] * W_SCALE[f]
            near = jnp.where(high_end, w[2][f], w[1][f])
            mid = jnp.where(high_end, w[1][f], w[2][f])
            far = jnp.where(high_end, w[0][f], w[3][f])
            part = (scale * D[3][2]) * near + (scale * D[3][1]) * mid + (scale * D[3][0]) * far
            faces[q, 5 + f] = jnp.where(high_end, part, -part)


def weights_of(lanes, high_end, spans):
    c_of = lanes // 8
    weight = jnp.where((c_of == 0) | (c_of == 3), 1.0 / 6.0, 5.0 / 6.0) / float(4 * spans)
    return jnp.where((lanes < 32) & jnp.logical_not(high_end), weight, 0.0)


def z_pack_kernel(spans, meta, st, own, left, right, opposite, zl, zh, ghosts, sums):
    n, inlet, outlet = place(meta)
    lanes, subs, low_half, high_end = masks()
    half = subs // 4
    used = lanes < 32
    for q in range(2):
        for v in range(9):
            lo = left[q, v]
            if v < 5:
                lo = jnp.where(inlet, pltpu.roll(opposite[q, v], 127, 1), lo)
            hi = right[q, v]
            if v < 5:
                hi = jnp.where(outlet, pltpu.roll(own[q, v], 1, 1), hi)
            ghosts[q, v] = jnp.where(used, jnp.where(high_end, lo, hi), 1.0)
    weight = weights_of(lanes, high_end, spans)
    last = n - 1
    last_q, last_half = last // 2, lax.rem(last, 2)
    for v in range(5):
        total = jnp.zeros((8, 128), F32)
        for q in range(2):
            total = total + jnp.where(2 * q + half < n, opposite[q, v] * weight, 0.0)
        sums[v] = total
        zl[77 + v] = total
        zh[77 + v] = total
        x = ghosts[0, v]
        zl[72 + v] = jnp.where(low_half, x, swap(x))
        x = ghosts[last_q, v]
        take_low = half == last_half
        zh[72 + v] = jnp.where(take_low, x, swap(x))

    dz = [[[JACOBS[2] * W_SCALE[f] * D[i][j] for j in range(4)] for i in range(4)] for f in range(4)]

    def rows(m, carry):
        for side, out in ((0, zl), (1, zh)):
            slot = 0 if side == 0 else last
            parts, states = [], []
            for ab in (m, m + 8):
                u0 = [st[slot, v, 2 * ab] for v in range(5)]
                u1 = [st[slot, v, 2 * ab + 1] for v in range(5)]
                w0, w1 = readings(to_prims(u0)), readings(to_prims(u1))
                part = []
                for f in range(4):
                    c = dz[f]
                    if side == 0:
                        x = jnp.where(low_half, 0.0, c[0][1]) * w0[f]
                        x = x + jnp.where(low_half, c[0][2], c[0][3]) * w1[f]
                    else:
                        x = jnp.where(low_half, c[3][0], c[3][1]) * w0[f]
                        x = x + jnp.where(low_half, c[3][2], 0.0) * w1[f]
                    part.append(x + swap(x))
                parts.append(part)
                states.append(u0 if side == 0 else u1)
            for v in range(5):
                if side == 0:
                    out[8 * v + m] = jnp.where(low_half, states[0][v], swap(states[1][v]))
                else:
                    out[8 * v + m] = jnp.where(low_half, swap(states[0][v]), states[1][v])
            for f in range(4):
                out[8 * (5 + f) + m] = jnp.where(low_half, parts[0][f], parts[1][f])
        return carry

    lax.fori_loop(0, 8, rows, 0)


def small_table(get, lanes, subs):
    b_of = lax.rem(lanes // 2, 4)
    y_of = lax.rem(subs, 4)
    acc = jnp.zeros((8, 128), F32)
    for b in range(4):
        for y in range(4):
            acc = jnp.where((b_of == b) & (y_of == y), get(b, y), acc)
    return acc


def profile_of(t, lanes, high_end):
    t = t + swap(t)
    t = t + pltpu.roll(t, 120, 1)
    t = t + pltpu.roll(t, 112, 1)
    t = jnp.where(lanes < 8, t, pltpu.roll(t, 8, 1))
    t = jnp.where(lanes < 16, t, pltpu.roll(t, 16, 1))
    return jnp.where(high_end, pltpu.roll(t, 127, 1), t)


def packed_derivative(w, step, index, low, high, scale):
    acc = jnp.where(index == 0, (-3.0 * scale) * low, jnp.where(index == 3, (3.0 * scale) * high, 0.0))
    for delta in (-3, -2, -1, 1, 2, 3):
        coefficient = jnp.zeros((8, 128), F32)
        for i in range(4):
            if 0 <= i + delta < 4:
                coefficient = jnp.where(index == i, scale * D[i][i + delta], coefficient)
        acc = acc + coefficient * pltpu.roll(w, (-delta * step) % 128, 1)
    return acc


GFIELDS = ((0, 1, 2, 6), (1, 3, 4, 7), (2, 4, 5, 8))


def main_kernel(
    meta, target, gain, st, own, opposite, ghosts, zfl, zfr, w4, s1, s2, s3,
    out, prim, xg, gx, zg, zgh, gz, gzh, part, grad, rate, gflux, rec, corner,
):
    n, inlet, outlet = place(meta)
    pairs = (n + 1) // 2
    lanes, subs, low_half, high_end = masks()
    y_of = lax.rem(subs, 4)
    half = subs // 4
    used = lanes < 32
    last_q = (n - 1) // 2
    even_n = lax.rem(n, 2) == 0

    gains = small_table(lambda b, y: gain[4 * b + y], lanes, subs)
    raw = [[], []]
    corners = [[], []]
    for v in range(5):
        profile = profile_of(w4[v] + s1[v] + s2[v] + s3[v], lanes, high_end)
        wanted = small_table(lambda b, y, v=v: target[16 * v + 4 * b + y], lanes, subs)
        for q in range(2):
            rec[q, v] = wanted + gains * (opposite[q, v] - profile)
            x = ghosts[q, v]
            raw[q].append(jnp.where(used, jnp.where(high_end, jnp.where(inlet, wanted + gains * (x - profile), x), x), 1.0))
        for side, src in enumerate((zfl, zfr)):
            x = src[72 + v]
            x = jnp.where(high_end, jnp.where(inlet, wanted + gains * (x - profile), x), x)
            corners[side].append(jnp.where(used, x, 1.0))
    for q in range(2):
        for f, x in enumerate(to_prims(raw[q])):
            xg[q, f] = x
    corner_w = [readings(to_prims(corners[side])) for side in range(2)]
    for f in range(4):
        corner[f] = jnp.where(low_half, pltpu.roll(corner_w[0][f], 104, 1), corner_w[1][f])

    own_w = [readings(to_prims([jnp.where(used, own[q, v], 1.0) for v in range(5)])) for q in range(2)]
    b_of, c_of = lax.rem(lanes // 2, 4), lanes // 8
    ghost_w = [[xg[q, HV], xg[q, HV + 1], xg[q, HV + 2], xg[q, TT]] for q in range(2)]
    for q in range(2):
        w = ghost_w[q]
        qx = []
        for f in range(4):
            o = own_w[q][f]
            o = (3.0 * JACOBS[0] * W_SCALE[f]) * jnp.where(high_end, pltpu.roll(o, 127, 1), pltpu.roll(o, 1, 1))
            qx.append(ghosts[q, 5 + f] + jnp.where(high_end, o, -o))
        dy = []
        for f in range(2):
            low = pltpu.roll(pltpu.roll(w[f], 122, 1), 1, 0)
            low = jnp.where(y_of == 0, -w[f], low)
            high = pltpu.roll(pltpu.roll(w[f], 6, 1), 7, 0)
            high = jnp.where(y_of == 3, w[f], high)
            dy.append(packed_derivative(w[f], 2, b_of, low, high, JACOBS[1] * W_SCALE[f]))
        dz = []
        slot = 2 * q + half
        for f in (0, 2):
            low = swap(jnp.where(low_half, w[f], ghost_w[max(q - 1, 0)][f]))
            low = pltpu.roll(jnp.where(slot == 0, corner_w[0][f], low), 104, 1)
            high = swap(jnp.where(low_half, ghost_w[min(q + 1, 1)][f], w[f]))
            high = pltpu.roll(jnp.where(slot == n - 1, corner_w[1][f], high), 24, 1)
            dz.append(packed_derivative(w[f], 8, c_of, low, high, JACOBS[2] * W_SCALE[f]))
        spread = (2.0 / 3.0) * (qx[0] + dy[1] + dz[1])
        t = [(qx[0] + qx[0]) - spread, qx[1] + dy[0], qx[2] + dz[0]]
        h = w[0] * t[0] + w[1] * t[1] + w[2] * t[2]
        for f, x in enumerate((*t, (h + h) + qx[3])):
            gx[q, f] = x

    def z_ghost(m, carry):
        first, second = [], []
        for v in range(9):
            a, b = zfl[8 * v + m], zfr[8 * v + m]
            first.append(jnp.where(low_half, a, swap(b)))
            second.append(jnp.where(low_half, swap(a), b))
        for ab, u in ((m, first), (m + 8, second)):
            for f, x in enumerate(to_prims(u[:5])):
                zg[f, ab] = x
                zgh[f, ab] = jnp.where(even_n, x, swap(x))
            for f in range(4):
                part[f, ab] = u[5 + f]
        return carry

    lax.fori_loop(0, 8, z_ghost, 0)

    def prims_of(q, carry):
        def nodes(kk, inner):
            first, second = [], []
            for v in range(5):
                a, b = st[2 * q, v, kk], st[2 * q + 1, v, kk]
                first.append(jnp.where(low_half, a, swap(b)))
                second.append(jnp.where(low_half, swap(a), b))
            for f, x in enumerate(to_prims(first)):
                prim[q, f, 2 * kk] = x
            for f, x in enumerate(to_prims(second)):
                prim[q, f, 2 * kk + 1] = x
            return inner

        return lax.fori_loop(0, 32, nodes, carry)

    lax.fori_loop(0, pairs, prims_of, 0)

    def ghost_lines(i, carry):
        at = [4 * j + i for j in range(4)]
        for k, f in enumerate((0, 2)):
            w = [zg[HV + f, at[j]] for j in range(4)]
            low = jnp.where(lanes == 0, packed(corner[f], 0, 2 * i), pltpu.roll(w[3], 1, 1))
            high = jnp.where(lanes == 127, packed(corner[f], 127, 2 * i + 1), pltpu.roll(w[0], 127, 1))
            for j, x in enumerate(line_derivative(w, low, high, JACOBS[0] * W_SCALE[f])):
                part[4 + k, at[j]] = x
        at = [4 * i + j for j in range(4)]
        for k, f in enumerate((1, 2)):
            w = [zg[HV + f, at[j]] for j in range(4)]
            low = jnp.where(y_of == 0, -w[0], pltpu.roll(w[3], 1, 0))
            high = jnp.where(y_of == 3, w[3], pltpu.roll(w[0], 7, 0))
            for j, x in enumerate(line_derivative(w, low, high, JACOBS[1] * W_SCALE[f])):
                part[6 + k, at[j]] = x
        return carry

    lax.fori_loop(0, 4, ghost_lines, 0)

    def ghost_flux(ab, carry):
        qz = []
        for f in range(4):
            src = HV + f if f < 3 else TT
            x = prim[last_q, src, 4 * ab + 3]
            o = jnp.where(low_half, prim[0, src, 4 * ab], jnp.where(even_n, x, swap(x)))
            o = (3.0 * JACOBS[2] * W_SCALE[f]) * o
            qz.append(part[f, ab] + jnp.where(low_half, o, -o))
        spread = (2.0 / 3.0) * (part[4, ab] + part[6, ab] + qz[2])
        t = [qz[0] + part[5, ab], qz[1] + part[7, ab], (qz[2] + qz[2]) - spread]
        h = zg[HV, ab] * t[0] + zg[HV + 1, ab] * t[1] + zg[HV + 2, ab] * t[2]
        for f, x in enumerate((*t, (h + h) + qz[3])):
            gz[f, ab] = x
            gzh[f, ab] = jnp.where(even_n, x, swap(x))
        return carry

    lax.fori_loop(0, 16, ghost_flux, 0)

    def direction(d):
        def per_pair(q, carry):
            slot = 2 * q + half
            before, after = jnp.maximum(q - 1, 0), jnp.minimum(q + 1, 1)

            def line(i, inner):
                base, stride = bases(d, i)
                at = [base + j * stride for j in range(4)]
                nodes = [[prim[q, f, at[j]] for f in range(NPRIM)] for j in range(4)]
                low, high = [], []
                if d == 0:
                    lane = lane_of(i)
                    for f in range(NPRIM):
                        ghost = packed(xg[q, f], 0, lane)
                        low.append(jnp.where(lanes == 0, ghost, pltpu.roll(nodes[3][f], 1, 1)))
                        ghost = packed(xg[q, f], 127, lane + 1)
                        high.append(
                            jnp.where(lanes == 127, ghost, pltpu.roll(nodes[0][f], 127, 1))
                        )
                elif d == 1:
                    for f in range(NPRIM):
                        wall = -nodes[0][f] if f == HV + 1 else nodes[0][f]
                        low.append(jnp.where(y_of == 0, wall, pltpu.roll(nodes[3][f], 1, 0)))
                        high.append(
                            jnp.where(y_of == 3, nodes[3][f], pltpu.roll(nodes[0][f], 7, 0))
                        )
                else:
                    for f in range(NPRIM):
                        prev, nxt = prim[before, f, at[3]], prim[after, f, at[0]]
                        x = swap(jnp.where(low_half, nodes[3][f], prev))
                        low.append(jnp.where(slot == 0, zg[f, i], x))
                        x = swap(jnp.where(low_half, nxt, nodes[0][f]))
                        high.append(jnp.where(slot == n - 1, zgh[f, i], x))
                change = line_inviscid(nodes, low, high, d)
                for j in range(4):
                    for v in range(5):
                        if d == 0:
                            rate[q, v, at[j]] = change[j][v]
                        else:
                            rate[q, v, at[j]] = rate[q, v, at[j]] + change[j][v]
                for k in range(4):
                    f = HV + k if k < 3 else TT
                    w_low = low[f]
                    if d == 1 and k in (0, 2):
                        w_low = jnp.where(y_of == 0, -nodes[0][f], w_low)
                    lifted = line_derivative(
                        [nodes[j][f] for j in range(4)], w_low, high[f], JACOBS[d] * W_SCALE[k]
                    )
                    for j in range(4):
                        grad[q, 4 * d + k, at[j]] = lifted[j]
                return inner

            return lax.fori_loop(0, 16, line, carry)

        lax.fori_loop(0, pairs, per_pair, 0)

    for d in range(3):
        direction(d)

    def fluxes(q, carry):
        def node(m, inner):
            e = [grad[q, k, m] for k in range(12)]
            hv = [prim[q, HV + k, m] for k in range(3)]
            spread = (2.0 / 3.0) * (e[0] + e[5] + e[10])
            t = {}
            for i in range(3):
                t[i, i] = (e[5 * i] + e[5 * i]) - spread
                for j in range(i + 1, 3):
                    t[i, j] = t[j, i] = e[4 * i + j] + e[4 * j + i]
            for index, key in enumerate(((0, 0), (0, 1), (0, 2), (1, 1), (1, 2), (2, 2))):
                gflux[q, index, m] = t[key]
            for i in range(3):
                h = hv[0] * t[i, 0] + hv[1] * t[i, 1] + hv[2] * t[i, 2]
                gflux[q, 6 + i, m] = (h + h) + e[4 * i + 3]
            return inner

        return lax.fori_loop(0, 64, node, carry)

    lax.fori_loop(0, pairs, fluxes, 0)

    def divergence(d):
        def per_pair(q, carry):
            slot = 2 * q + half
            before, after = jnp.maximum(q - 1, 0), jnp.minimum(q + 1, 1)

            def line(i, inner):
                base, stride = bases(d, i)
                at = [base + j * stride for j in range(4)]
                g = [[gflux[q, f, at[j]] for f in GFIELDS[d]] for j in range(4)]
                low, high = [], []
                if d == 0:
                    lane = lane_of(i)
                    inner_low = list(g[0])
                    for k in range(3):
                        dv = packed(xg[q, HV + k], 0, lane) - prim[q, HV + k, at[0]]
                        inner_low[3] = inner_low[3] + (dv + dv) * g[0][k]
                    for f in range(4):
                        ghost = packed(gx[q, f], 0, lane)
                        ghost = jnp.where(inlet, inner_low[f], ghost)
                        low.append(jnp.where(lanes == 0, ghost, pltpu.roll(g[3][f], 1, 1)))
                        ghost = packed(gx[q, f], 127, lane + 1)
                        ghost = jnp.where(outlet, g[3][f], ghost)
                        high.append(jnp.where(lanes == 127, ghost, pltpu.roll(g[0][f], 127, 1)))
                elif d == 1:
                    for f in range(4):
                        low.append(jnp.where(y_of == 0, g[0][f], pltpu.roll(g[3][f], 1, 0)))
                        high.append(jnp.where(y_of == 3, g[3][f], pltpu.roll(g[0][f], 7, 0)))
                else:
                    for f in range(4):
                        src = GFIELDS[d][f]
                        prev, nxt = gflux[before, src, at[3]], gflux[after, src, at[0]]
                        x = swap(jnp.where(low_half, g[3][f], prev))
                        low.append(jnp.where(slot == 0, gz[f, i], x))
                        x = swap(jnp.where(low_half, nxt, g[0][f]))
                        high.append(jnp.where(slot == n - 1, gzh[f, i], x))
                for f in range(4):
                    change = line_derivative(
                        [g[j][f] for j in range(4)], low[f], high[f], JACOBS[d] * STEP_DT
                    )
                    for j in range(4):
                        rate[q, f + 1, at[j]] = rate[q, f + 1, at[j]] + change[j]
                return inner

            return lax.fori_loop(0, 16, line, carry)

        lax.fori_loop(0, pairs, per_pair, 0)

    for d in range(3):
        divergence(d)

    for q in range(2):

        @pl.when(2 * q < n)
        def _(q=q):
            second = 2 * q + 1 < n

            def relax(i, carry):
                lane = lane_of(i) + 1
                for v in range(5):
                    step = (STEP_DT * RELAX) * (rec[q, v] - own[q, v])
                    x = packed(step, 0, lane)
                    rate[q, v, i] = rate[q, v, i] + jnp.where(lanes == 0, x, 0.0)
                return carry

            lax.fori_loop(0, 16, relax, 0)

            def nodes(kk, carry):
                for v in range(5):
                    x, y = rate[q, v, 2 * kk], rate[q, v, 2 * kk + 1]
                    out[2 * q, v, kk] = st[2 * q, v, kk] + jnp.where(low_half, x, swap(y))
                    b = st[2 * q + 1, v, kk]
                    z = b + jnp.where(low_half, swap(x), y)
                    out[2 * q + 1, v, kk] = jnp.where(second, z, b)
                return carry

            lax.fori_loop(0, 32, nodes, 0)

        @pl.when(2 * q >= n)
        def _(q=q):
            out[2 * q] = st[2 * q]
            out[2 * q + 1] = st[2 * q + 1]


def shape(*dims):
    return jax.ShapeDtypeStruct(dims, F32)


def vspec():
    return pl.BlockSpec(memory_space=pltpu.VMEM)


def sspec():
    return pl.BlockSpec(memory_space=pltpu.SMEM)


PARAMS = pltpu.CompilerParams(vmem_limit_bytes=56 << 20)


def shifted(array, axis, by):
    count = lax.axis_size(axis)
    return lax.ppermute(array, axis, [(i, (i + by) % count) for i in range(count)])


def vmem(*dims):
    return pltpu.VMEM(dims, F32)


def on_device(state, columns, target_profile, fluct_gain):
    st = state.reshape(4, 5, 32, 8, 128)
    streams, spans = lax.axis_size("stream"), lax.axis_size("span")
    n = lax.dynamic_index_in_dim(columns, lax.axis_index("span"), 0, keepdims=False)
    meta = jnp.stack([lax.axis_index("stream"), jnp.int32(streams), n])
    own = pl.pallas_call(
        pack_kernel,
        out_shape=shape(2, 9, 8, 128),
        in_specs=[vspec()],
        out_specs=vspec(),
        scratch_shapes=[vmem(2, 4, 5, 8, 128)],
        compiler_params=PARAMS,
        name="x_faces",
    )(st)
    left = shifted(own, "stream", 1)
    right = shifted(own, "stream", -1)
    opposite = shifted(own, "stream", streams // 2)
    zl, zh, ghosts, sums = pl.pallas_call(
        functools.partial(z_pack_kernel, spans),
        out_shape=(shape(82, 8, 128), shape(82, 8, 128), shape(2, 9, 8, 128), shape(5, 8, 128)),
        in_specs=[sspec()] + [vspec()] * 5,
        out_specs=(vspec(),) * 4,
        compiler_params=PARAMS,
        name="z_faces",
    )(meta, st, own, left, right, opposite)
    zfl = shifted(zh, "span", 1)
    zfr = shifted(zl, "span", -1)
    w4 = sums + zfl[77:82] + zfr[77:82] + shifted(sums, "span", -2)
    s1, s2, s3 = (shifted(w4, "span", k) for k in (4, 8, 12))
    target, gain = target_profile.reshape(-1), fluct_gain.reshape(-1)
    out = pl.pallas_call(
        main_kernel,
        out_shape=shape(4, 5, 32, 8, 128),
        in_specs=[sspec()] * 3 + [vspec()] * 10,
        out_specs=vspec(),
        scratch_shapes=[
            vmem(2, NPRIM, 64, 8, 128),
            vmem(2, NPRIM, 8, 128),
            vmem(2, 4, 8, 128),
            vmem(NPRIM, 16, 8, 128),
            vmem(NPRIM, 16, 8, 128),
            vmem(4, 16, 8, 128),
            vmem(4, 16, 8, 128),
            vmem(8, 16, 8, 128),
            vmem(2, 12, 64, 8, 128),
            vmem(2, 5, 64, 8, 128),
            vmem(2, 9, 64, 8, 128),
            vmem(2, 5, 8, 128),
            vmem(4, 8, 128),
        ],
        compiler_params=PARAMS,
        name="section",
    )(meta, target, gain, st, own, opposite, ghosts, zfl, zfr, w4, s1, s2, s3)
    return out.reshape(state.shape)


def solution(mesh):
    placed = (P("span", None, None, None, "stream"), P(), P(), P())
    return jax.shard_map(
        on_device,
        mesh=mesh,
        in_specs=placed,
        out_specs=P("span", None, None, None, "stream"),
        check_vma=False,
    )
```

```python
import functools
import math

import jax
import jax.numpy as jnp
from jax import lax
from jax.experimental import pallas as pl
from jax.experimental.pallas import tpu as pltpu
from jax.sharding import PartitionSpec as P

GAMMA = 1.4
VISC = 0.02
COND = VISC * GAMMA / (GAMMA - 1.0) / 0.72
JACOBS = (5.0, 10.0, 5.0)
STEP_DT = 0.004
RELAX = 10.0
HR, HV, HP, HE, TT, HC = 0, 1, 4, 5, 6, 7
NPRIM = 8
F32 = jnp.float32


def derivative_table():
    inner_node = math.sqrt(0.2)
    points = [-1.0, -inner_node, inner_node, 1.0]
    barycentric = []
    for j in range(4):
        product = 1.0
        for k in range(4):
            if k != j:
                product = product * (points[j] - points[k])
        barycentric.append(1.0 / product)
    entries = [[0.0] * 4 for _ in range(4)]
    for i in range(4):
        diagonal = 0.0
        for j in range(4):
            if i != j:
                entries[i][j] = barycentric[j] / barycentric[i] / (points[i] - points[j])
                diagonal = diagonal - entries[i][j]
        entries[i][i] = diagonal
    return entries


D = derivative_table()
Q = [[(1.0 / 6.0, 5.0 / 6.0, 5.0 / 6.0, 1.0 / 6.0)[i] * D[i][j] for j in range(4)] for i in range(4)]


def lane_iota():
    return lax.broadcasted_iota(jnp.int32, (8, 128), 1)


def sub_iota():
    return lax.broadcasted_iota(jnp.int32, (8, 128), 0)


def swap(x):
    return pltpu.roll(x, 4, 0)


def lane_of(node):
    return 8 * (node % 4) + 2 * (node // 4)


def bases(d, i):
    if d == 0:
        return i, 16
    if d == 1:
        return 16 * (i // 4) + i % 4, 4
    return 4 * i, 1


def to_prims(u):
    inv = 1.0 / u[0]
    hv = [(0.5 * u[k + 1]) * inv for k in range(3)]
    kin = u[1] * hv[0] + u[2] * hv[1] + u[3] * hv[2]
    hp = (0.5 * (GAMMA - 1.0)) * (u[4] - kin)
    he = (0.5 * u[4]) * inv
    temp = (2.0 * hp) * inv
    hc = 0.5 * jnp.sqrt(GAMMA * temp)
    return [0.5 * u[0], *hv, hp, he, temp, hc]


def pair_terms(left, right, d, scale):
    kr = scale * (left[HR] + right[HR])
    vel = [left[HV + k] + right[HV + k] for k in range(3)]
    kp = scale * (left[HP] + right[HP])
    he = left[HE] + right[HE]
    carried = kr * vel[d]
    out = [carried]
    for k in range(3):
        entry = carried * vel[k]
        if k == d:
            entry = entry + kp
        out.append(entry)
    out.append(carried * he + kp * vel[d])
    return out


def face_terms(left, right, d, scale):
    flux = pair_terms(left, right, d, scale)
    speed = jnp.maximum(jnp.abs(left[HV + d]) + left[HC], jnp.abs(right[HV + d]) + right[HC])
    two = (2.0 * scale) * speed
    four = two + two
    out = [flux[0] - two * (right[HR] - left[HR])]
    for k in range(3):
        out.append(flux[k + 1] - four * (right[HR] * right[HV + k] - left[HR] * left[HV + k]))
    out.append(flux[4] - four * (right[HR] * right[HE] - left[HR] * left[HE]))
    return out


def line_inviscid(nodes, f_low, f_high, d):
    scale = 2.4 * JACOBS[d] * STEP_DT
    g = {}
    for i in range(4):
        for j in range(i + 1, 4):
            g[i, j] = pair_terms(nodes[i], nodes[j], d, scale * Q[i][j])
    r0 = [5.0 * (f_low[v] - g[0, 1][v] - g[0, 2][v] - g[0, 3][v]) for v in range(5)]
    r1 = [g[0, 1][v] - g[1, 2][v] - g[1, 3][v] for v in range(5)]
    r2 = [g[0, 2][v] + g[1, 2][v] - g[2, 3][v] for v in range(5)]
    r3 = [5.0 * (g[0, 3][v] + g[1, 3][v] + g[2, 3][v] - f_high[v]) for v in range(5)]
    return r0, r1, r2, r3


def line_derivative(w, low, high, scale):
    c = [[scale * D[i][j] for j in range(4)] for i in range(4)]
    three = 3.0 * scale
    return (
        c[0][1] * w[1] + c[0][2] * w[2] + c[0][3] * w[3] - three * low,
        c[1][0] * w[0] + c[1][2] * w[2] + c[1][3] * w[3],
        c[2][0] * w[0] + c[2][1] * w[1] + c[2][3] * w[3],
        c[3][0] * w[0] + c[3][1] * w[1] + c[3][2] * w[2] + three * high,
    )


def packed(value, at_lane, lane):
    return pltpu.roll(value, lax.rem(at_lane + 128 - lane, 128), 1)


def masks():
    lanes, subs = lane_iota(), sub_iota()
    return lanes, subs, subs < 4, lax.rem(lanes, 2) == 0


def place(axes_ref):
    n = axes_ref[2]
    return n, axes_ref[0] == 0, axes_ref[0] == axes_ref[1] - 1


W_SCALE = (2.0 * VISC, 2.0 * VISC, 2.0 * VISC, COND)


def readings(prims):
    return [prims[HV], prims[HV + 1], prims[HV + 2], prims[TT]]


def pack_kernel(st, faces, planes):
    lanes, subs, low_half, high_end = masks()
    even_c = lax.rem(lanes // 8, 2) == 0

    def per_field(v, carry):
        for a in range(4):
            gathered = []
            for s in range(4):
                acc = jnp.ones((8, 128), F32)
                for k in range(8):
                    target = 16 * (k % 2) + 2 * (k // 2)
                    moved = pltpu.roll(st[s, v, 8 * a + k], target + 1, 1)
                    acc = jnp.where(lanes // 2 == target // 2, moved, acc)
                gathered.append(acc)
            for q in range(2):
                za, zb = gathered[2 * q], gathered[2 * q + 1]
                even = jnp.where(low_half, za, swap(zb))
                odd = jnp.where(low_half, swap(za), zb)
                planes[q, a, v] = jnp.where(even_c, even, pltpu.roll(odd, 8, 1))
        return carry

    lax.fori_loop(0, 5, per_field, 0)
    for q in range(2):
        w = []
        for a in range(4):
            w.append(readings(to_prims([planes[q, a, v] for v in range(5)])))
        for v in range(5):
            faces[q, v] = jnp.where(high_end, planes[q, 3, v], planes[q, 0, v])
        for f in range(4):
            scale = JACOBS[0] * W_SCALE[f]
            near = jnp.where(high_end, w[2][f], w[1][f])
            mid = jnp.where(high_end, w[1][f], w[2][f])
            far = jnp.where(high_end, w[0][f], w[3][f])
            part = (scale * D[3][2]) * near + (scale * D[3][1]) * mid + (scale * D[3][0]) * far
            faces[q, 5 + f] = jnp.where(high_end, part, -part)


def weights_of(lanes, high_end, spans):
    c_of = lanes // 8
    weight = jnp.where((c_of == 0) | (c_of == 3), 1.0 / 6.0, 5.0 / 6.0) / float(4 * spans)
    return jnp.where((lanes < 32) & jnp.logical_not(high_end), weight, 0.0)


def z_pack_kernel(spans, meta, st, own, left, right, opposite, zl, zh, ghosts, sums):
    n, inlet, outlet = place(meta)
    lanes, subs, low_half, high_end = masks()
    half = subs // 4
    used = lanes < 32
    for q in range(2):
        for v in range(9):
            lo, hi = pltpu.roll(left[q, v], 1, 1), pltpu.roll(right[q, v], 127, 1)
            if v < 5:
                lo = jnp.where(inlet, opposite[q, v], lo)
                hi = jnp.where(outlet, own[q, v], hi)
            ghosts[q, v] = jnp.where(used, jnp.where(high_end, hi, lo), 1.0)
    weight = weights_of(lanes, high_end, spans)
    last = n - 1
    last_q, last_half = last // 2, lax.rem(last, 2)
    for v in range(5):
        total = jnp.zeros((8, 128), F32)
        for q in range(2):
            total = total + jnp.where(2 * q + half < n, opposite[q, v] * weight, 0.0)
        sums[v] = total
        zl[77 + v] = total
        zh[77 + v] = total
        x = ghosts[0, v]
        zl[72 + v] = jnp.where(low_half, x, swap(x))
        x = ghosts[last_q, v]
        take_low = half == last_half
        zh[72 + v] = jnp.where(take_low, x, swap(x))

    dz = [[[JACOBS[2] * W_SCALE[f] * D[i][j] for j in range(4)] for i in range(4)] for f in range(4)]

    def rows(m, carry):
        for side, out in ((0, zl), (1, zh)):
            slot = 0 if side == 0 else last
            parts, states = [], []
            for ab in (m, m + 8):
                u0 = [st[slot, v, 2 * ab] for v in range(5)]
                u1 = [st[slot, v, 2 * ab + 1] for v in range(5)]
                w0, w1 = readings(to_prims(u0)), readings(to_prims(u1))
                part = []
                for f in range(4):
                    c = dz[f]
                    if side == 0:
                        x = jnp.where(low_half, 0.0, c[0][1]) * w0[f]
                        x = x + jnp.where(low_half, c[0][2], c[0][3]) * w1[f]
                    else:
                        x = jnp.where(low_half, c[3][0], c[3][1]) * w0[f]
                        x = x + jnp.where(low_half, c[3][2], 0.0) * w1[f]
                    part.append(x + swap(x))
                parts.append(part)
                states.append(u0 if side == 0 else u1)
            for v in range(5):
                if side == 0:
                    out[8 * v + m] = jnp.where(low_half, states[0][v], swap(states[1][v]))
                else:
                    out[8 * v + m] = jnp.where(low_half, swap(states[0][v]), states[1][v])
            for f in range(4):
                out[8 * (5 + f) + m] = jnp.where(low_half, parts[0][f], parts[1][f])
        return carry

    lax.fori_loop(0, 8, rows, 0)


def small_table(get, lanes, subs):
    b_of = lax.rem(lanes // 2, 4)
    y_of = lax.rem(subs, 4)
    acc = jnp.zeros((8, 128), F32)
    for b in range(4):
        for y in range(4):
            acc = jnp.where((b_of == b) & (y_of == y), get(b, y), acc)
    return acc


def profile_of(t, lanes, high_end):
    t = t + swap(t)
    t = t + pltpu.roll(t, 120, 1)
    t = t + pltpu.roll(t, 112, 1)
    t = jnp.where(lanes < 8, t, pltpu.roll(t, 8, 1))
    t = jnp.where(lanes < 16, t, pltpu.roll(t, 16, 1))
    return jnp.where(high_end, pltpu.roll(t, 127, 1), t)


def packed_derivative(w, step, index, low, high, scale):
    acc = jnp.where(index == 0, (-3.0 * scale) * low, jnp.where(index == 3, (3.0 * scale) * high, 0.0))
    for delta in (-3, -2, -1, 1, 2, 3):
        coefficient = jnp.zeros((8, 128), F32)
        for i in range(4):
            if 0 <= i + delta < 4:
                coefficient = jnp.where(index == i, scale * D[i][i + delta], coefficient)
        acc = acc + coefficient * pltpu.roll(w, (-delta * step) % 128, 1)
    return acc


GFIELDS = ((0, 1, 2, 6), (1, 3, 4, 7), (2, 4, 5, 8))


def main_kernel(
    meta, target, gain, st, own, opposite, ghosts, zfl, zfr, w4, s1, s2, s3,
    out, prim, xg, gx, fx, zg, zgh, gz, gzh, part, grad, rate, gflux, rec, corner,
):
    n, inlet, outlet = place(meta)
    pairs = (n + 1) // 2
    lanes, subs, low_half, high_end = masks()
    y_of = lax.rem(subs, 4)
    half = subs // 4
    used = lanes < 32
    last_q = (n - 1) // 2
    even_n = lax.rem(n, 2) == 0

    gains = small_table(lambda b, y: gain[4 * b + y], lanes, subs)
    raw = [[], []]
    corners = [[], []]
    for v in range(5):
        profile = profile_of(w4[v] + s1[v] + s2[v] + s3[v], lanes, high_end)
        wanted = small_table(lambda b, y, v=v: target[16 * v + 4 * b + y], lanes, subs)
        for q in range(2):
            rec[q, v] = wanted + gains * (opposite[q, v] - profile)
            x = ghosts[q, v]
            y = jnp.where(inlet, wanted + gains * (x - profile), x)
            raw[q].append(jnp.where(used, jnp.where(high_end, x, y), 1.0))
        for side, src in enumerate((zfl, zfr)):
            x = src[72 + v]
            y = jnp.where(inlet, wanted + gains * (x - profile), x)
            x = jnp.where(high_end, x, y)
            corners[side].append(jnp.where(used, x, 1.0))
    for q in range(2):
        for f, x in enumerate(to_prims(raw[q])):
            xg[q, f] = x
    corner_w = [readings(to_prims(corners[side])) for side in range(2)]
    for f in range(4):
        corner[f] = jnp.where(low_half, pltpu.roll(corner_w[0][f], 104, 1), corner_w[1][f])

    own_p = [to_prims([jnp.where(used, own[q, v], 1.0) for v in range(5)]) for q in range(2)]
    b_of, c_of = lax.rem(lanes // 2, 4), lanes // 8
    ghost_w = [[xg[q, HV], xg[q, HV + 1], xg[q, HV + 2], xg[q, TT]] for q in range(2)]
    for q in range(2):
        w = ghost_w[q]
        qx = []
        for f in range(4):
            o = (3.0 * JACOBS[0] * W_SCALE[f]) * readings(own_p[q])[f]
            qx.append(ghosts[q, 5 + f] + jnp.where(high_end, -o, o))
        dy = []
        for f in range(2):
            low = pltpu.roll(pltpu.roll(w[f], 122, 1), 1, 0)
            low = jnp.where(y_of == 0, -w[f], low)
            high = pltpu.roll(pltpu.roll(w[f], 6, 1), 7, 0)
            high = jnp.where(y_of == 3, w[f], high)
            dy.append(packed_derivative(w[f], 2, b_of, low, high, JACOBS[1] * W_SCALE[f]))
        dz = []
        slot = 2 * q + half
        for f in (0, 2):
            low = swap(jnp.where(low_half, w[f], ghost_w[max(q - 1, 0)][f]))
            low = pltpu.roll(jnp.where(slot == 0, corner_w[0][f], low), 104, 1)
            high = swap(jnp.where(low_half, ghost_w[min(q + 1, 1)][f], w[f]))
            high = pltpu.roll(jnp.where(slot == n - 1, corner_w[1][f], high), 24, 1)
            dz.append(packed_derivative(w[f], 8, c_of, low, high, JACOBS[2] * W_SCALE[f]))
        spread = (2.0 / 3.0) * (qx[0] + dy[1] + dz[1])
        t = [(qx[0] + qx[0]) - spread, qx[1] + dy[0], qx[2] + dz[0]]
        h = w[0] * t[0] + w[1] * t[1] + w[2] * t[2]
        for f, x in enumerate((*t, (h + h) + qx[3])):
            gx[q, f] = x
        for k in range(3):
            x = xg[q, HV + k] - own_p[q][HV + k]
            gx[q, 4 + k] = x + x
        ghost = [xg[q, f] for f in range(NPRIM)]
        first = [jnp.where(high_end, own_p[q][f], ghost[f]) for f in range(NPRIM)]
        second = [jnp.where(high_end, ghost[f], own_p[q][f]) for f in range(NPRIM)]
        for v, x in enumerate(face_terms(first, second, 0, 1.2 * JACOBS[0] * STEP_DT)):
            step = (0.2 * STEP_DT * RELAX) * (rec[q, v] - own[q, v])
            fx[q, v] = x + jnp.where(high_end, 0.0, step)

    def z_ghost(m, carry):
        first, second = [], []
        for v in range(9):
            a, b = zfl[8 * v + m], zfr[8 * v + m]
            first.append(jnp.where(low_half, a, swap(b)))
            second.append(jnp.where(low_half, swap(a), b))
        for ab, u in ((m, first), (m + 8, second)):
            for f, x in enumerate(to_prims(u[:5])):
                zg[f, ab] = x
                zgh[f, ab] = jnp.where(even_n, x, swap(x))
            for f in range(4):
                part[f, ab] = u[5 + f]
        return carry

    lax.fori_loop(0, 8, z_ghost, 0, unroll=2)

    def prims_of(q, carry):
        def nodes(kk, inner):
            first, second = [], []
            for v in range(5):
                a, b = st[2 * q, v, kk], st[2 * q + 1, v, kk]
                first.append(jnp.where(low_half, a, swap(b)))
                second.append(jnp.where(low_half, swap(a), b))
            for f, x in enumerate(to_prims(first)):
                prim[q, f, 2 * kk] = x
            for f, x in enumerate(to_prims(second)):
                prim[q, f, 2 * kk + 1] = x
            return inner

        return lax.fori_loop(0, 32, nodes, carry, unroll=2)

    lax.fori_loop(0, pairs, prims_of, 0)

    def ghost_lines(i, carry):
        at = [4 * j + i for j in range(4)]
        for k, f in enumerate((0, 2)):
            w = [zg[HV + f, at[j]] for j in range(4)]
            ghost = pltpu.roll(corner[f], 127 - 2 * i, 1)
            low = jnp.where(lanes == 0, ghost, pltpu.roll(w[3], 1, 1))
            high = jnp.where(lanes == 127, ghost, pltpu.roll(w[0], 127, 1))
            for j, x in enumerate(line_derivative(w, low, high, JACOBS[0] * W_SCALE[f])):
                part[4 + k, at[j]] = x
        at = [4 * i + j for j in range(4)]
        for k, f in enumerate((1, 2)):
            w = [zg[HV + f, at[j]] for j in range(4)]
            low = jnp.where(y_of == 0, -w[0], pltpu.roll(w[3], 1, 0))
            high = jnp.where(y_of == 3, w[3], pltpu.roll(w[0], 7, 0))
            for j, x in enumerate(line_derivative(w, low, high, JACOBS[1] * W_SCALE[f])):
                part[6 + k, at[j]] = x
        return carry

    for i in range(4):
        ghost_lines(i, 0)

    def ghost_flux(ab, carry):
        qz = []
        for f in range(4):
            src = HV + f if f < 3 else TT
            x = prim[last_q, src, 4 * ab + 3]
            o = jnp.where(low_half, prim[0, src, 4 * ab], jnp.where(even_n, x, swap(x)))
            o = (3.0 * JACOBS[2] * W_SCALE[f]) * o
            qz.append(part[f, ab] + jnp.where(low_half, o, -o))
        spread = (2.0 / 3.0) * (part[4, ab] + part[6, ab] + qz[2])
        t = [qz[0] + part[5, ab], qz[1] + part[7, ab], (qz[2] + qz[2]) - spread]
        h = zg[HV, ab] * t[0] + zg[HV + 1, ab] * t[1] + zg[HV + 2, ab] * t[2]
        for f, x in enumerate((*t, (h + h) + qz[3])):
            gz[f, ab] = x
            gzh[f, ab] = jnp.where(even_n, x, swap(x))
        return carry

    lax.fori_loop(0, 16, ghost_flux, 0, unroll=4)

    FIELDS = (HR, HV, HV + 1, HV + 2, HP, HE, HC)
    W_FIELDS = (HV, HV + 1, HV + 2, TT)

    def direction(d):
        scale = 1.2 * JACOBS[d] * STEP_DT

        def per_pair(q, carry):
            slot = 2 * q + half
            before, after = jnp.maximum(q - 1, 0), jnp.minimum(q + 1, 1)

            def line(i, inner):
                base, stride = bases(d, i)
                at = [base + j * stride for j in range(4)]
                nodes = [[prim[q, f, at[j]] for f in range(NPRIM)] for j in range(4)]
                low, high = {}, {}
                if d == 0:
                    shift = 127 - lane_of(i)
                    for f in FIELDS:
                        low[f] = pltpu.roll(nodes[3][f], 1, 1)
                    f_low = face_terms(low, nodes[0], d, scale)
                    f_high = []
                    for v in range(5):
                        ghost = pltpu.roll(fx[q, v], shift, 1)
                        f_high.append(
                            jnp.where(lanes == 127, ghost, pltpu.roll(f_low[v], 127, 1))
                        )
                        f_low[v] = jnp.where(lanes == 0, ghost, f_low[v])
                    for f in W_FIELDS:
                        ghost = pltpu.roll(xg[q, f], shift, 1)
                        x = pltpu.roll(nodes[3][f], 1, 1) if f == TT else low[f]
                        low[f] = jnp.where(lanes == 0, ghost, x)
                        high[f] = jnp.where(lanes == 127, ghost, pltpu.roll(nodes[0][f], 127, 1))
                elif d == 1:
                    for f in FIELDS:
                        wall = -nodes[0][f] if f == HV + 1 else nodes[0][f]
                        low[f] = jnp.where(y_of == 0, wall, pltpu.roll(nodes[3][f], 1, 0))
                    f_low = face_terms(low, nodes[0], d, scale)
                    top = pair_terms(nodes[3], nodes[3], d, scale)
                    f_high = [
                        jnp.where(y_of == 3, top[v], pltpu.roll(f_low[v], 7, 0)) for v in range(5)
                    ]
                    for f in W_FIELDS:
                        if f == TT:
                            low[f] = jnp.where(y_of == 0, nodes[0][f], pltpu.roll(nodes[3][f], 1, 0))
                        elif f != HV + 1:
                            low[f] = jnp.where(y_of == 0, -nodes[0][f], low[f])
                        high[f] = jnp.where(y_of == 3, nodes[3][f], pltpu.roll(nodes[0][f], 7, 0))
                else:
                    for f in range(NPRIM):
                        prev, nxt = prim[before, f, at[3]], prim[after, f, at[0]]
                        x = swap(jnp.where(low_half, nodes[3][f], prev))
                        low[f] = jnp.where(slot == 0, zg[f, i], x)
                        x = swap(jnp.where(low_half, nxt, nodes[0][f]))
                        high[f] = jnp.where(slot == n - 1, zgh[f, i], x)
                    f_low = face_terms(low, nodes[0], d, scale)
                    f_high = face_terms(nodes[3], high, d, scale)
                change = line_inviscid(nodes, f_low, f_high, d)
                for j in range(4):
                    for v in range(5):
                        if d == 0:
                            rate[q, v, at[j]] = change[j][v]
                        else:
                            rate[q, v, at[j]] = rate[q, v, at[j]] + change[j][v]
                for k, f in enumerate(W_FIELDS):
                    lifted = line_derivative(
                        [nodes[j][f] for j in range(4)], low[f], high[f], JACOBS[d] * W_SCALE[k]
                    )
                    for j in range(4):
                        grad[q, 4 * d + k, at[j]] = lifted[j]
                return inner

            if d == 0:
                for i in range(16):
                    line(i, 0)
                return carry
            return lax.fori_loop(0, 16, line, carry, unroll=2)

        lax.fori_loop(0, pairs, per_pair, 0)

    for d in range(3):
        direction(d)

    def fluxes(q, carry):
        def node(m, inner):
            e = [grad[q, k, m] for k in range(12)]
            hv = [prim[q, HV + k, m] for k in range(3)]
            spread = (2.0 / 3.0) * (e[0] + e[5] + e[10])
            t = {}
            for i in range(3):
                t[i, i] = (e[5 * i] + e[5 * i]) - spread
                for j in range(i + 1, 3):
                    t[i, j] = t[j, i] = e[4 * i + j] + e[4 * j + i]
            for index, key in enumerate(((0, 0), (0, 1), (0, 2), (1, 1), (1, 2), (2, 2))):
                gflux[q, index, m] = t[key]
            for i in range(3):
                h = hv[0] * t[i, 0] + hv[1] * t[i, 1] + hv[2] * t[i, 2]
                gflux[q, 6 + i, m] = (h + h) + e[4 * i + 3]
            return inner

        return lax.fori_loop(0, 64, node, carry, unroll=4)

    lax.fori_loop(0, pairs, fluxes, 0)

    def divergence(d):
        def per_pair(q, carry):
            slot = 2 * q + half
            before, after = jnp.maximum(q - 1, 0), jnp.minimum(q + 1, 1)
            second = 2 * q + 1 < n

            def line(i, inner):
                base, stride = bases(d, i)
                at = [base + j * stride for j in range(4)]
                g = [[gflux[q, f, at[j]] for f in GFIELDS[d]] for j in range(4)]
                low, high = [], []
                if d == 0:
                    shift = 127 - lane_of(i)
                    inner_low = list(g[0])
                    for k in range(3):
                        inner_low[3] = inner_low[3] + pltpu.roll(gx[q, 4 + k], shift, 1) * g[0][k]
                    for f in range(4):
                        ghost = pltpu.roll(gx[q, f], shift, 1)
                        x = jnp.where(inlet, inner_low[f], ghost)
                        low.append(jnp.where(lanes == 0, x, pltpu.roll(g[3][f], 1, 1)))
                        x = jnp.where(outlet, g[3][f], ghost)
                        high.append(jnp.where(lanes == 127, x, pltpu.roll(g[0][f], 127, 1)))
                elif d == 1:
                    for f in range(4):
                        low.append(jnp.where(y_of == 0, g[0][f], pltpu.roll(g[3][f], 1, 0)))
                        high.append(jnp.where(y_of == 3, g[3][f], pltpu.roll(g[0][f], 7, 0)))
                else:
                    for f in range(4):
                        src = GFIELDS[d][f]
                        prev, nxt = gflux[before, src, at[3]], gflux[after, src, at[0]]
                        x = swap(jnp.where(low_half, g[3][f], prev))
                        low.append(jnp.where(slot == 0, gz[f, i], x))
                        x = swap(jnp.where(low_half, nxt, g[0][f]))
                        high.append(jnp.where(slot == n - 1, gzh[f, i], x))
                total = [[rate[q, 0, at[j]] for j in range(4)]] if d == 2 else []
                for f in range(4):
                    change = line_derivative(
                        [g[j][f] for j in range(4)], low[f], high[f], JACOBS[d] * STEP_DT
                    )
                    if d == 2:
                        total.append([rate[q, f + 1, at[j]] + change[j] for j in range(4)])
                    else:
                        for j in range(4):
                            rate[q, f + 1, at[j]] = rate[q, f + 1, at[j]] + change[j]
                if d == 2:
                    for v in range(5):
                        for m in range(2):
                            x, y = total[v][2 * m], total[v][2 * m + 1]
                            kk = 2 * i + m
                            out[2 * q, v, kk] = st[2 * q, v, kk] + jnp.where(low_half, x, swap(y))
                            b = st[2 * q + 1, v, kk]
                            z = b + jnp.where(low_half, swap(x), y)
                            out[2 * q + 1, v, kk] = jnp.where(second, z, b)
                return inner

            if d == 0:
                for i in range(16):
                    line(i, 0)
                return carry
            return lax.fori_loop(0, 16, line, carry, unroll=2)

        lax.fori_loop(0, pairs, per_pair, 0)

    for d in range(3):
        divergence(d)

    @pl.when(pairs == 1)
    def _():
        out[2] = st[2]
        out[3] = st[3]


def shape(*dims):
    return jax.ShapeDtypeStruct(dims, F32)


def vspec():
    return pl.BlockSpec(memory_space=pltpu.VMEM)


def sspec():
    return pl.BlockSpec(memory_space=pltpu.SMEM)


PARAMS = pltpu.CompilerParams(vmem_limit_bytes=56 << 20)


def shifted(array, axis, by):
    count = lax.axis_size(axis)
    return lax.ppermute(array, axis, [(i, (i + by) % count) for i in range(count)])


def vmem(*dims):
    return pltpu.VMEM(dims, F32)


def on_device(state, columns, target_profile, fluct_gain):
    st = state.reshape(4, 5, 32, 8, 128)
    streams, spans = lax.axis_size("stream"), lax.axis_size("span")
    n = lax.dynamic_index_in_dim(columns, lax.axis_index("span"), 0, keepdims=False)
    meta = jnp.stack([lax.axis_index("stream"), jnp.int32(streams), n])
    own = pl.pallas_call(
        pack_kernel,
        out_shape=shape(2, 9, 8, 128),
        in_specs=[vspec()],
        out_specs=vspec(),
        scratch_shapes=[vmem(2, 4, 5, 8, 128)],
        compiler_params=PARAMS,
        name="x_faces",
    )(st)
    left = shifted(own, "stream", 1)
    right = shifted(own, "stream", -1)
    opposite = shifted(own, "stream", streams // 2)
    zl, zh, ghosts, sums = pl.pallas_call(
        functools.partial(z_pack_kernel, spans),
        out_shape=(shape(82, 8, 128), shape(82, 8, 128), shape(2, 9, 8, 128), shape(5, 8, 128)),
        in_specs=[sspec()] + [vspec()] * 5,
        out_specs=(vspec(),) * 4,
        compiler_params=PARAMS,
        name="z_faces",
    )(meta, st, own, left, right, opposite)
    zfl = shifted(zh, "span", 1)
    zfr = shifted(zl, "span", -1)
    w4 = sums + zfl[77:82] + zfr[77:82] + shifted(sums, "span", -2)
    s1, s2, s3 = (shifted(w4, "span", k) for k in (4, 8, 12))
    target, gain = target_profile.reshape(-1), fluct_gain.reshape(-1)
    out = pl.pallas_call(
        main_kernel,
        out_shape=shape(4, 5, 32, 8, 128),
        in_specs=[sspec()] * 3 + [vspec()] * 10,
        out_specs=vspec(),
        scratch_shapes=[
            vmem(2, NPRIM, 64, 8, 128),
            vmem(2, NPRIM, 8, 128),
            vmem(2, 7, 8, 128),
            vmem(2, 5, 8, 128),
            vmem(NPRIM, 16, 8, 128),
            vmem(NPRIM, 16, 8, 128),
            vmem(4, 16, 8, 128),
            vmem(4, 16, 8, 128),
            vmem(8, 16, 8, 128),
            vmem(2, 12, 64, 8, 128),
            vmem(2, 5, 64, 8, 128),
            vmem(2, 9, 64, 8, 128),
            vmem(2, 5, 8, 128),
            vmem(4, 8, 128),
        ],
        compiler_params=PARAMS,
        name="section",
    )(meta, target, gain, st, own, opposite, ghosts, zfl, zfr, w4, s1, s2, s3)
    return out.reshape(state.shape)


def solution(mesh):
    placed = (P("span", None, None, None, "stream"), P(), P(), P())
    return jax.shard_map(
        on_device,
        mesh=mesh,
        in_specs=placed,
        out_specs=P("span", None, None, None, "stream"),
        check_vma=False,
    )
```

```python
import functools
import math

import jax
import jax.numpy as jnp
from jax import lax
from jax.experimental import pallas as pl
from jax.experimental.pallas import tpu as pltpu
from jax.sharding import PartitionSpec as P

GAMMA = 1.4
VISC = 0.02
COND = VISC * GAMMA / (GAMMA - 1.0) / 0.72
JACOBS = (5.0, 10.0, 5.0)
STEP_DT = 0.004
RELAX = 10.0
HR, HV, HP, HE, TT, HC = 0, 1, 4, 5, 6, 7
NPRIM = 8
F32 = jnp.float32


def derivative_table():
    inner_node = math.sqrt(0.2)
    points = [-1.0, -inner_node, inner_node, 1.0]
    barycentric = []
    for j in range(4):
        product = 1.0
        for k in range(4):
            if k != j:
                product = product * (points[j] - points[k])
        barycentric.append(1.0 / product)
    entries = [[0.0] * 4 for _ in range(4)]
    for i in range(4):
        diagonal = 0.0
        for j in range(4):
            if i != j:
                entries[i][j] = barycentric[j] / barycentric[i] / (points[i] - points[j])
                diagonal = diagonal - entries[i][j]
        entries[i][i] = diagonal
    return entries


D = derivative_table()
Q = [[(1.0 / 6.0, 5.0 / 6.0, 5.0 / 6.0, 1.0 / 6.0)[i] * D[i][j] for j in range(4)] for i in range(4)]


def lane_iota():
    return lax.broadcasted_iota(jnp.int32, (8, 128), 1)


def sub_iota():
    return lax.broadcasted_iota(jnp.int32, (8, 128), 0)


def swap(x):
    return pltpu.roll(x, 4, 0)


def lane_of(node):
    return 8 * (node % 4) + 2 * (node // 4)


def bases(d, i):
    if d == 0:
        return i, 16
    if d == 1:
        return 16 * (i // 4) + i % 4, 4
    return 4 * i, 1


def to_prims(u):
    inv = 1.0 / u[0]
    hv = [(0.5 * u[k + 1]) * inv for k in range(3)]
    kin = u[1] * hv[0] + u[2] * hv[1] + u[3] * hv[2]
    hp = (0.5 * (GAMMA - 1.0)) * (u[4] - kin)
    he = (0.5 * u[4]) * inv
    temp = (2.0 * hp) * inv
    hc = 0.5 * jnp.sqrt(GAMMA * temp)
    return [0.5 * u[0], *hv, hp, he, temp, hc]


def pair_terms(left, right, d, scale):
    kr = scale * (left[HR] + right[HR])
    vel = [left[HV + k] + right[HV + k] for k in range(3)]
    kp = scale * (left[HP] + right[HP])
    he = left[HE] + right[HE]
    carried = kr * vel[d]
    out = [carried]
    for k in range(3):
        entry = carried * vel[k]
        if k == d:
            entry = entry + kp
        out.append(entry)
    out.append(carried * he + kp * vel[d])
    return out


def face_terms(left, right, d, scale):
    flux = pair_terms(left, right, d, scale)
    speed = jnp.maximum(jnp.abs(left[HV + d]) + left[HC], jnp.abs(right[HV + d]) + right[HC])
    two = (2.0 * scale) * speed
    four = two + two
    out = [flux[0] - two * (right[HR] - left[HR])]
    for k in range(3):
        out.append(flux[k + 1] - four * (right[HR] * right[HV + k] - left[HR] * left[HV + k]))
    out.append(flux[4] - four * (right[HR] * right[HE] - left[HR] * left[HE]))
    return out


def line_inviscid(nodes, f_low, f_high, d):
    scale = 2.4 * JACOBS[d] * STEP_DT
    g = {}
    for i in range(4):
        for j in range(i + 1, 4):
            g[i, j] = pair_terms(nodes[i], nodes[j], d, scale * Q[i][j])
    r0 = [5.0 * (f_low[v] - g[0, 1][v] - g[0, 2][v] - g[0, 3][v]) for v in range(5)]
    r1 = [g[0, 1][v] - g[1, 2][v] - g[1, 3][v] for v in range(5)]
    r2 = [g[0, 2][v] + g[1, 2][v] - g[2, 3][v] for v in range(5)]
    r3 = [5.0 * (g[0, 3][v] + g[1, 3][v] + g[2, 3][v] - f_high[v]) for v in range(5)]
    return r0, r1, r2, r3


def line_derivative(w, low, high, scale):
    c = [[scale * D[i][j] for j in range(4)] for i in range(4)]
    three = 3.0 * scale
    return (
        c[0][1] * w[1] + c[0][2] * w[2] + c[0][3] * w[3] - three * low,
        c[1][0] * w[0] + c[1][2] * w[2] + c[1][3] * w[3],
        c[2][0] * w[0] + c[2][1] * w[1] + c[2][3] * w[3],
        c[3][0] * w[0] + c[3][1] * w[1] + c[3][2] * w[2] + three * high,
    )


def packed(value, at_lane, lane):
    return pltpu.roll(value, lax.rem(at_lane + 128 - lane, 128), 1)


def masks():
    lanes, subs = lane_iota(), sub_iota()
    return lanes, subs, subs < 4, lax.rem(lanes, 2) == 0


def place(columns):
    n = columns[lax.axis_index("span")]
    stream = lax.axis_index("stream")
    return n, stream == 0, stream == lax.axis_size("stream") - 1


W_SCALE = (2.0 * VISC, 2.0 * VISC, 2.0 * VISC, COND)


def readings(prims):
    return [prims[HV], prims[HV + 1], prims[HV + 2], prims[TT]]


def weights_of(lanes, high_end, spans):
    c_of = lanes // 8
    weight = jnp.where((c_of == 0) | (c_of == 3), 1.0 / 6.0, 5.0 / 6.0) / float(4 * spans)
    return jnp.where((lanes < 32) & jnp.logical_not(high_end), weight, 0.0)


def plane_sums(spans, n, faces, sums):
    lanes, subs, _, high_end = masks()
    weight = weights_of(lanes, high_end, spans)
    for v in range(5):
        total = jnp.zeros((8, 128), F32)
        for q in range(2):
            total = total + jnp.where(2 * q + subs // 4 < n, faces[q, v] * weight, 0.0)
        sums[v] = total


def pack_kernel(spans, columns, st, faces, sums, planes):
    lanes, subs, low_half, high_end = masks()
    n, _, _ = place(columns)
    even_c = lax.rem(lanes // 8, 2) == 0

    def per_field(v, carry):
        for a in range(4):
            gathered = []
            for s in range(4):
                acc = jnp.ones((8, 128), F32)
                for k in range(8):
                    target = 16 * (k % 2) + 2 * (k // 2)
                    moved = pltpu.roll(st[s, v, 8 * a + k], target + 1, 1)
                    acc = jnp.where(lanes // 2 == target // 2, moved, acc)
                gathered.append(acc)
            for q in range(2):
                za, zb = gathered[2 * q], gathered[2 * q + 1]
                even = jnp.where(low_half, za, swap(zb))
                odd = jnp.where(low_half, swap(za), zb)
                planes[q, a, v] = jnp.where(even_c, even, pltpu.roll(odd, 8, 1))
        return carry

    lax.fori_loop(0, 5, per_field, 0)
    for q in range(2):
        w = []
        for a in range(4):
            w.append(readings(to_prims([planes[q, a, v] for v in range(5)])))
        for v in range(5):
            faces[q, v] = jnp.where(high_end, planes[q, 3, v], planes[q, 0, v])
        for f in range(4):
            scale = JACOBS[0] * W_SCALE[f]
            near = jnp.where(high_end, w[2][f], w[1][f])
            mid = jnp.where(high_end, w[1][f], w[2][f])
            far = jnp.where(high_end, w[0][f], w[3][f])
            part = (scale * D[3][2]) * near + (scale * D[3][1]) * mid + (scale * D[3][0]) * far
            faces[q, 5 + f] = jnp.where(high_end, part, -part)
    plane_sums(spans, n, faces, sums)


def z_pack_kernel(spans, meta, st, own, left, right, opposite, s1, s2, s3, zl, zh, ghosts, sums):
    n, inlet, outlet = place(meta)
    lanes, subs, low_half, high_end = masks()
    half = subs // 4
    used = lanes < 32
    for q in range(2):
        for v in range(9):
            lo, hi = pltpu.roll(left[q, v], 1, 1), pltpu.roll(right[q, v], 127, 1)
            if v < 5:
                lo = jnp.where(inlet, opposite[q, v], lo)
                hi = jnp.where(outlet, own[q, v], hi)
            ghosts[q, v] = jnp.where(used, jnp.where(high_end, hi, lo), 1.0)
    plane_sums(spans, n, opposite, sums)
    last = n - 1
    last_q, last_half = last // 2, lax.rem(last, 2)
    for v in range(5):
        total = sums[v] + s1[v] + s2[v] + s3[v]
        sums[v] = total
        zl[77 + v] = total
        zh[77 + v] = total
        x = ghosts[0, v]
        zl[72 + v] = jnp.where(low_half, x, swap(x))
        x = ghosts[last_q, v]
        take_low = half == last_half
        zh[72 + v] = jnp.where(take_low, x, swap(x))

    dz = [[[JACOBS[2] * W_SCALE[f] * D[i][j] for j in range(4)] for i in range(4)] for f in range(4)]

    def rows(m, carry):
        for side, out in ((0, zl), (1, zh)):
            slot = 0 if side == 0 else last
            parts, states = [], []
            for ab in (m, m + 8):
                u0 = [st[slot, v, 2 * ab] for v in range(5)]
                u1 = [st[slot, v, 2 * ab + 1] for v in range(5)]
                w0, w1 = readings(to_prims(u0)), readings(to_prims(u1))
                part = []
                for f in range(4):
                    c = dz[f]
                    if side == 0:
                        x = jnp.where(low_half, 0.0, c[0][1]) * w0[f]
                        x = x + jnp.where(low_half, c[0][2], c[0][3]) * w1[f]
                    else:
                        x = jnp.where(low_half, c[3][0], c[3][1]) * w0[f]
                        x = x + jnp.where(low_half, c[3][2], 0.0) * w1[f]
                    part.append(x + swap(x))
                parts.append(part)
                states.append(u0 if side == 0 else u1)
            for v in range(5):
                if side == 0:
                    out[8 * v + m] = jnp.where(low_half, states[0][v], swap(states[1][v]))
                else:
                    out[8 * v + m] = jnp.where(low_half, swap(states[0][v]), states[1][v])
            for f in range(4):
                out[8 * (5 + f) + m] = jnp.where(low_half, parts[0][f], parts[1][f])
        return carry

    lax.fori_loop(0, 8, rows, 0)


def small_table(get, lanes, subs):
    b_of = lax.rem(lanes // 2, 4)
    y_of = lax.rem(subs, 4)
    acc = jnp.zeros((8, 128), F32)
    for b in range(4):
        for y in range(4):
            acc = jnp.where((b_of == b) & (y_of == y), get(b, y), acc)
    return acc


def profile_of(t, lanes, high_end):
    t = t + swap(t)
    t = t + pltpu.roll(t, 120, 1)
    t = t + pltpu.roll(t, 112, 1)
    t = jnp.where(lanes < 8, t, pltpu.roll(t, 8, 1))
    t = jnp.where(lanes < 16, t, pltpu.roll(t, 16, 1))
    return jnp.where(high_end, pltpu.roll(t, 127, 1), t)


def packed_derivative(w, step, index, low, high, scale):
    acc = jnp.where(index == 0, (-3.0 * scale) * low, jnp.where(index == 3, (3.0 * scale) * high, 0.0))
    for delta in (-3, -2, -1, 1, 2, 3):
        coefficient = jnp.zeros((8, 128), F32)
        for i in range(4):
            if 0 <= i + delta < 4:
                coefficient = jnp.where(index == i, scale * D[i][i + delta], coefficient)
        acc = acc + coefficient * pltpu.roll(w, (-delta * step) % 128, 1)
    return acc


GFIELDS = ((0, 1, 2, 6), (1, 3, 4, 7), (2, 4, 5, 8))


def main_kernel(
    meta, target, gain, st, own, opposite, ghosts, zfl, zfr, w4, s2,
    out, prim, xg, gx, fx, zg, zgh, gz, gzh, part, grad, rate, gflux, rec, corner,
):
    n, inlet, outlet = place(meta)
    pairs = (n + 1) // 2
    lanes, subs, low_half, high_end = masks()
    y_of = lax.rem(subs, 4)
    half = subs // 4
    used = lanes < 32
    last_q = (n - 1) // 2
    even_n = lax.rem(n, 2) == 0

    gains = small_table(lambda b, y: gain[b, y], lanes, subs)
    raw = [[], []]
    corners = [[], []]
    for v in range(5):
        profile = profile_of(w4[v] + s2[v] + zfl[77 + v] + zfr[77 + v], lanes, high_end)
        wanted = small_table(lambda b, y, v=v: target[v, b, y], lanes, subs)
        for q in range(2):
            rec[q, v] = wanted + gains * (opposite[q, v] - profile)
            x = ghosts[q, v]
            y = jnp.where(inlet, wanted + gains * (x - profile), x)
            raw[q].append(jnp.where(used, jnp.where(high_end, x, y), 1.0))
        for side, src in enumerate((zfl, zfr)):
            x = src[72 + v]
            y = jnp.where(inlet, wanted + gains * (x - profile), x)
            x = jnp.where(high_end, x, y)
            corners[side].append(jnp.where(used, x, 1.0))
    for q in range(2):
        for f, x in enumerate(to_prims(raw[q])):
            xg[q, f] = x
    corner_w = [readings(to_prims(corners[side])) for side in range(2)]
    for f in range(4):
        corner[f] = jnp.where(low_half, pltpu.roll(corner_w[0][f], 104, 1), corner_w[1][f])

    own_p = [to_prims([jnp.where(used, own[q, v], 1.0) for v in range(5)]) for q in range(2)]
    b_of, c_of = lax.rem(lanes // 2, 4), lanes // 8
    ghost_w = [[xg[q, HV], xg[q, HV + 1], xg[q, HV + 2], xg[q, TT]] for q in range(2)]
    for q in range(2):
        w = ghost_w[q]
        qx = []
        for f in range(4):
            o = (3.0 * JACOBS[0] * W_SCALE[f]) * readings(own_p[q])[f]
            qx.append(ghosts[q, 5 + f] + jnp.where(high_end, -o, o))
        dy = []
        for f in range(2):
            low = pltpu.roll(pltpu.roll(w[f], 122, 1), 1, 0)
            low = jnp.where(y_of == 0, -w[f], low)
            high = pltpu.roll(pltpu.roll(w[f], 6, 1), 7, 0)
            high = jnp.where(y_of == 3, w[f], high)
            dy.append(packed_derivative(w[f], 2, b_of, low, high, JACOBS[1] * W_SCALE[f]))
        dz = []
        slot = 2 * q + half
        for f in (0, 2):
            low = swap(jnp.where(low_half, w[f], ghost_w[max(q - 1, 0)][f]))
            low = pltpu.roll(jnp.where(slot == 0, corner_w[0][f], low), 104, 1)
            high = swap(jnp.where(low_half, ghost_w[min(q + 1, 1)][f], w[f]))
            high = pltpu.roll(jnp.where(slot == n - 1, corner_w[1][f], high), 24, 1)
            dz.append(packed_derivative(w[f], 8, c_of, low, high, JACOBS[2] * W_SCALE[f]))
        spread = (2.0 / 3.0) * (qx[0] + dy[1] + dz[1])
        t = [(qx[0] + qx[0]) - spread, qx[1] + dy[0], qx[2] + dz[0]]
        h = w[0] * t[0] + w[1] * t[1] + w[2] * t[2]
        for f, x in enumerate((*t, (h + h) + qx[3])):
            gx[q, f] = x
        for k in range(3):
            x = xg[q, HV + k] - own_p[q][HV + k]
            gx[q, 4 + k] = x + x
        ghost = [xg[q, f] for f in range(NPRIM)]
        first = [jnp.where(high_end, own_p[q][f], ghost[f]) for f in range(NPRIM)]
        second = [jnp.where(high_end, ghost[f], own_p[q][f]) for f in range(NPRIM)]
        for v, x in enumerate(face_terms(first, second, 0, 1.2 * JACOBS[0] * STEP_DT)):
            step = (0.2 * STEP_DT * RELAX) * (rec[q, v] - own[q, v])
            fx[q, v] = x + jnp.where(high_end, 0.0, step)

    def z_ghost(m, carry):
        first, second = [], []
        for v in range(9):
            a, b = zfl[8 * v + m], zfr[8 * v + m]
            first.append(jnp.where(low_half, a, swap(b)))
            second.append(jnp.where(low_half, swap(a), b))
        for ab, u in ((m, first), (m + 8, second)):
            for f, x in enumerate(to_prims(u[:5])):
                zg[f, ab] = x
                zgh[f, ab] = jnp.where(even_n, x, swap(x))
            for f in range(4):
                part[f, ab] = u[5 + f]
        return carry

    lax.fori_loop(0, 8, z_ghost, 0, unroll=2)

    def prims_of(q, carry):
        def nodes(kk, inner):
            first, second = [], []
            for v in range(5):
                a, b = st[2 * q, v, kk], st[2 * q + 1, v, kk]
                first.append(jnp.where(low_half, a, swap(b)))
                second.append(jnp.where(low_half, swap(a), b))
            for f, x in enumerate(to_prims(first)):
                prim[q, f, 2 * kk] = x
            for f, x in enumerate(to_prims(second)):
                prim[q, f, 2 * kk + 1] = x
            return inner

        return lax.fori_loop(0, 32, nodes, carry, unroll=2)

    lax.fori_loop(0, pairs, prims_of, 0)

    def ghost_lines(i, carry):
        at = [4 * j + i for j in range(4)]
        for k, f in enumerate((0, 2)):
            w = [zg[HV + f, at[j]] for j in range(4)]
            ghost = pltpu.roll(corner[f], 127 - 2 * i, 1)
            low = jnp.where(lanes == 0, ghost, pltpu.roll(w[3], 1, 1))
            high = jnp.where(lanes == 127, ghost, pltpu.roll(w[0], 127, 1))
            for j, x in enumerate(line_derivative(w, low, high, JACOBS[0] * W_SCALE[f])):
                part[4 + k, at[j]] = x
        at = [4 * i + j for j in range(4)]
        for k, f in enumerate((1, 2)):
            w = [zg[HV + f, at[j]] for j in range(4)]
            low = jnp.where(y_of == 0, -w[0], pltpu.roll(w[3], 1, 0))
            high = jnp.where(y_of == 3, w[3], pltpu.roll(w[0], 7, 0))
            for j, x in enumerate(line_derivative(w, low, high, JACOBS[1] * W_SCALE[f])):
                part[6 + k, at[j]] = x
        return carry

    for i in range(4):
        ghost_lines(i, 0)

    def ghost_flux(ab, carry):
        qz = []
        for f in range(4):
            src = HV + f if f < 3 else TT
            x = prim[last_q, src, 4 * ab + 3]
            o = jnp.where(low_half, prim[0, src, 4 * ab], jnp.where(even_n, x, swap(x)))
            o = (3.0 * JACOBS[2] * W_SCALE[f]) * o
            qz.append(part[f, ab] + jnp.where(low_half, o, -o))
        spread = (2.0 / 3.0) * (part[4, ab] + part[6, ab] + qz[2])
        t = [qz[0] + part[5, ab], qz[1] + part[7, ab], (qz[2] + qz[2]) - spread]
        h = zg[HV, ab] * t[0] + zg[HV + 1, ab] * t[1] + zg[HV + 2, ab] * t[2]
        for f, x in enumerate((*t, (h + h) + qz[3])):
            gz[f, ab] = x
            gzh[f, ab] = jnp.where(even_n, x, swap(x))
        return carry

    lax.fori_loop(0, 16, ghost_flux, 0, unroll=4)

    FIELDS = (HR, HV, HV + 1, HV + 2, HP, HE, HC)
    W_FIELDS = (HV, HV + 1, HV + 2, TT)

    def direction(d):
        scale = 1.2 * JACOBS[d] * STEP_DT

        def per_pair(q, carry):
            slot = 2 * q + half
            before, after = jnp.maximum(q - 1, 0), jnp.minimum(q + 1, 1)

            def line(i, inner):
                base, stride = bases(d, i)
                at = [base + j * stride for j in range(4)]
                nodes = [[prim[q, f, at[j]] for f in range(NPRIM)] for j in range(4)]
                low, high = {}, {}
                if d == 0:
                    shift = 127 - lane_of(i)
                    for f in FIELDS:
                        low[f] = pltpu.roll(nodes[3][f], 1, 1)
                    f_low = face_terms(low, nodes[0], d, scale)
                    f_high = []
                    for v in range(5):
                        ghost = pltpu.roll(fx[q, v], shift, 1)
                        f_high.append(
                            jnp.where(lanes == 127, ghost, pltpu.roll(f_low[v], 127, 1))
                        )
                        f_low[v] = jnp.where(lanes == 0, ghost, f_low[v])
                    for f in W_FIELDS:
                        ghost = pltpu.roll(xg[q, f], shift, 1)
                        x = pltpu.roll(nodes[3][f], 1, 1) if f == TT else low[f]
                        low[f] = jnp.where(lanes == 0, ghost, x)
                        high[f] = jnp.where(lanes == 127, ghost, pltpu.roll(nodes[0][f], 127, 1))
                elif d == 1:
                    for f in FIELDS:
                        wall = -nodes[0][f] if f == HV + 1 else nodes[0][f]
                        low[f] = jnp.where(y_of == 0, wall, pltpu.roll(nodes[3][f], 1, 0))
                    f_low = face_terms(low, nodes[0], d, scale)
                    top = pair_terms(nodes[3], nodes[3], d, scale)
                    f_high = [
                        jnp.where(y_of == 3, top[v], pltpu.roll(f_low[v], 7, 0)) for v in range(5)
                    ]
                    for f in W_FIELDS:
                        if f == TT:
                            low[f] = jnp.where(y_of == 0, nodes[0][f], pltpu.roll(nodes[3][f], 1, 0))
                        elif f != HV + 1:
                            low[f] = jnp.where(y_of == 0, -nodes[0][f], low[f])
                        high[f] = jnp.where(y_of == 3, nodes[3][f], pltpu.roll(nodes[0][f], 7, 0))
                else:
                    for f in range(NPRIM):
                        prev, nxt = prim[before, f, at[3]], prim[after, f, at[0]]
                        x = swap(jnp.where(low_half, nodes[3][f], prev))
                        low[f] = jnp.where(slot == 0, zg[f, i], x)
                        x = swap(jnp.where(low_half, nxt, nodes[0][f]))
                        high[f] = jnp.where(slot == n - 1, zgh[f, i], x)
                    f_low = face_terms(low, nodes[0], d, scale)
                    f_high = face_terms(nodes[3], high, d, scale)
                change = line_inviscid(nodes, f_low, f_high, d)
                for j in range(4):
                    for v in range(5):
                        if d == 0:
                            rate[q, v, at[j]] = change[j][v]
                        else:
                            rate[q, v, at[j]] = rate[q, v, at[j]] + change[j][v]
                for k, f in enumerate(W_FIELDS):
                    lifted = line_derivative(
                        [nodes[j][f] for j in range(4)], low[f], high[f], JACOBS[d] * W_SCALE[k]
                    )
                    for j in range(4):
                        grad[q, 4 * d + k, at[j]] = lifted[j]
                return inner

            if d == 0:
                for i in range(16):
                    line(i, 0)
                return carry
            return lax.fori_loop(0, 16, line, carry, unroll=2)

        lax.fori_loop(0, pairs, per_pair, 0)

    for d in range(3):
        direction(d)

    def fluxes(q, carry):
        def node(m, inner):
            e = [grad[q, k, m] for k in range(12)]
            hv = [prim[q, HV + k, m] for k in range(3)]
            spread = (2.0 / 3.0) * (e[0] + e[5] + e[10])
            t = {}
            for i in range(3):
                t[i, i] = (e[5 * i] + e[5 * i]) - spread
                for j in range(i + 1, 3):
                    t[i, j] = t[j, i] = e[4 * i + j] + e[4 * j + i]
            for index, key in enumerate(((0, 0), (0, 1), (0, 2), (1, 1), (1, 2), (2, 2))):
                gflux[q, index, m] = t[key]
            for i in range(3):
                h = hv[0] * t[i, 0] + hv[1] * t[i, 1] + hv[2] * t[i, 2]
                gflux[q, 6 + i, m] = (h + h) + e[4 * i + 3]
            return inner

        return lax.fori_loop(0, 64, node, carry, unroll=4)

    lax.fori_loop(0, pairs, fluxes, 0)

    def divergence(d):
        def per_pair(q, carry):
            slot = 2 * q + half
            before, after = jnp.maximum(q - 1, 0), jnp.minimum(q + 1, 1)
            second = 2 * q + 1 < n

            def line(i, inner):
                base, stride = bases(d, i)
                at = [base + j * stride for j in range(4)]
                g = [[gflux[q, f, at[j]] for f in GFIELDS[d]] for j in range(4)]
                low, high = [], []
                if d == 0:
                    shift = 127 - lane_of(i)
                    inner_low = list(g[0])
                    for k in range(3):
                        inner_low[3] = inner_low[3] + pltpu.roll(gx[q, 4 + k], shift, 1) * g[0][k]
                    for f in range(4):
                        ghost = pltpu.roll(gx[q, f], shift, 1)
                        x = jnp.where(inlet, inner_low[f], ghost)
                        low.append(jnp.where(lanes == 0, x, pltpu.roll(g[3][f], 1, 1)))
                        x = jnp.where(outlet, g[3][f], ghost)
                        high.append(jnp.where(lanes == 127, x, pltpu.roll(g[0][f], 127, 1)))
                elif d == 1:
                    for f in range(4):
                        low.append(jnp.where(y_of == 0, g[0][f], pltpu.roll(g[3][f], 1, 0)))
                        high.append(jnp.where(y_of == 3, g[3][f], pltpu.roll(g[0][f], 7, 0)))
                else:
                    for f in range(4):
                        src = GFIELDS[d][f]
                        prev, nxt = gflux[before, src, at[3]], gflux[after, src, at[0]]
                        x = swap(jnp.where(low_half, g[3][f], prev))
                        low.append(jnp.where(slot == 0, gz[f, i], x))
                        x = swap(jnp.where(low_half, nxt, g[0][f]))
                        high.append(jnp.where(slot == n - 1, gzh[f, i], x))
                total = [[rate[q, 0, at[j]] for j in range(4)]] if d == 2 else []
                for f in range(4):
                    change = line_derivative(
                        [g[j][f] for j in range(4)], low[f], high[f], JACOBS[d] * STEP_DT
                    )
                    if d == 2:
                        total.append([rate[q, f + 1, at[j]] + change[j] for j in range(4)])
                    else:
                        for j in range(4):
                            rate[q, f + 1, at[j]] = rate[q, f + 1, at[j]] + change[j]
                if d == 2:
                    for v in range(5):
                        for m in range(2):
                            x, y = total[v][2 * m], total[v][2 * m + 1]
                            kk = 2 * i + m
                            out[2 * q, v, kk] = st[2 * q, v, kk] + jnp.where(low_half, x, swap(y))
                            b = st[2 * q + 1, v, kk]
                            z = b + jnp.where(low_half, swap(x), y)
                            out[2 * q + 1, v, kk] = jnp.where(second, z, b)
                return inner

            if d == 0:
                for i in range(16):
                    line(i, 0)
                return carry
            return lax.fori_loop(0, 16, line, carry, unroll=2)

        lax.fori_loop(0, pairs, per_pair, 0)

    for d in range(3):
        divergence(d)

    @pl.when(pairs == 1)
    def _():
        out[2] = st[2]
        out[3] = st[3]


def shape(*dims):
    return jax.ShapeDtypeStruct(dims, F32)


def vspec():
    return pl.BlockSpec(memory_space=pltpu.VMEM)


def sspec():
    return pl.BlockSpec(memory_space=pltpu.SMEM)


def params(mib):
    return pltpu.CompilerParams(vmem_limit_bytes=mib << 20)


def shifted(array, axis, by):
    count = lax.axis_size(axis)
    return lax.ppermute(array, axis, [(i, (i + by) % count) for i in range(count)])


def opposite_shifted(array, by):
    streams, spans = lax.axis_size("stream"), lax.axis_size("span")
    pairs = []
    for i in range(streams):
        for p in range(spans):
            to = (i + streams // 2) % streams * spans + (p - by) % spans
            pairs.append((i * spans + p, to))
    return lax.ppermute(array, ("stream", "span"), pairs)


def vmem(*dims):
    return pltpu.VMEM(dims, F32)


def on_device(state, columns, target_profile, fluct_gain):
    st = state.reshape(4, 5, 32, 8, 128)
    streams, spans = lax.axis_size("stream"), lax.axis_size("span")
    own, part = pl.pallas_call(
        functools.partial(pack_kernel, spans),
        out_shape=(shape(2, 9, 8, 128), shape(5, 8, 128)),
        in_specs=[sspec(), vspec()],
        out_specs=(vspec(), vspec()),
        scratch_shapes=[vmem(2, 4, 5, 8, 128)],
        compiler_params=params(8),
        name="x_faces",
    )(columns, st)
    left = shifted(own, "stream", 1)
    right = shifted(own, "stream", -1)
    opposite = shifted(own, "stream", streams // 2)
    s1, s2, s3 = (opposite_shifted(part, k) for k in (4, 8, 12))
    zl, zh, ghosts, w4 = pl.pallas_call(
        functools.partial(z_pack_kernel, spans),
        out_shape=(shape(82, 8, 128), shape(82, 8, 128), shape(2, 9, 8, 128), shape(5, 8, 128)),
        in_specs=[sspec()] + [vspec()] * 8,
        out_specs=(vspec(),) * 4,
        compiler_params=params(8),
        name="z_faces",
    )(columns, st, own, left, right, opposite, s1, s2, s3)
    zfl = shifted(zh, "span", 1)
    zfr = shifted(zl, "span", -1)
    s2 = shifted(w4, "span", -2)
    out = pl.pallas_call(
        main_kernel,
        out_shape=shape(4, 5, 32, 8, 128),
        in_specs=[sspec()] * 3 + [vspec()] * 8,
        out_specs=vspec(),
        scratch_shapes=[
            vmem(2, NPRIM, 64, 8, 128),
            vmem(2, NPRIM, 8, 128),
            vmem(2, 7, 8, 128),
            vmem(2, 5, 8, 128),
            vmem(NPRIM, 16, 8, 128),
            vmem(NPRIM, 16, 8, 128),
            vmem(4, 16, 8, 128),
            vmem(4, 16, 8, 128),
            vmem(8, 16, 8, 128),
            vmem(2, 12, 64, 8, 128),
            vmem(2, 5, 64, 8, 128),
            vmem(2, 9, 64, 8, 128),
            vmem(2, 5, 8, 128),
            vmem(4, 8, 128),
        ],
        compiler_params=params(30),
        name="section",
    )(columns, target_profile, fluct_gain, st, own, opposite, ghosts, zfl, zfr, w4, s2)
    return out.reshape(state.shape)


def solution(mesh):
    placed = (P("span", None, None, None, "stream"), P(), P(), P())
    return jax.shard_map(
        on_device,
        mesh=mesh,
        in_specs=placed,
        out_specs=P("span", None, None, None, "stream"),
        check_vma=False,
    )
```

```python
import functools
import math

import jax
import jax.numpy as jnp
from jax import lax
from jax.experimental import pallas as pl
from jax.experimental.pallas import tpu as pltpu
from jax.sharding import PartitionSpec as P

GAMMA = 1.4
VISC = 0.02
COND = VISC * GAMMA / (GAMMA - 1.0) / 0.72
JACOBS = (5.0, 10.0, 5.0)
STEP_DT = 0.004
RELAX = 10.0
HR, HV, HP, HE, TT, HC = 0, 1, 4, 5, 6, 7
NPRIM = 8
F32 = jnp.float32


def derivative_table():
    inner_node = math.sqrt(0.2)
    points = [-1.0, -inner_node, inner_node, 1.0]
    barycentric = []
    for j in range(4):
        product = 1.0
        for k in range(4):
            if k != j:
                product = product * (points[j] - points[k])
        barycentric.append(1.0 / product)
    entries = [[0.0] * 4 for _ in range(4)]
    for i in range(4):
        diagonal = 0.0
        for j in range(4):
            if i != j:
                entries[i][j] = barycentric[j] / barycentric[i] / (points[i] - points[j])
                diagonal = diagonal - entries[i][j]
        entries[i][i] = diagonal
    return entries


D = derivative_table()
Q = [[(1.0 / 6.0, 5.0 / 6.0, 5.0 / 6.0, 1.0 / 6.0)[i] * D[i][j] for j in range(4)] for i in range(4)]


def lane_iota():
    return lax.broadcasted_iota(jnp.int32, (8, 128), 1)


def sub_iota():
    return lax.broadcasted_iota(jnp.int32, (8, 128), 0)


def swap(x):
    return pltpu.roll(x, 4, 0)


def lane_of(node):
    return 8 * (node % 4) + 2 * (node // 4)


def bases(d, i):
    if d == 0:
        return i, 16
    if d == 1:
        return 16 * (i // 4) + i % 4, 4
    return 4 * i, 1


def to_prims(u):
    inv = 1.0 / u[0]
    hv = [(0.5 * u[k + 1]) * inv for k in range(3)]
    kin = u[1] * hv[0] + u[2] * hv[1] + u[3] * hv[2]
    hp = (0.5 * (GAMMA - 1.0)) * (u[4] - kin)
    he = (0.5 * u[4]) * inv
    temp = (2.0 * hp) * inv
    hc = 0.5 * jnp.sqrt(GAMMA * temp)
    return [0.5 * u[0], *hv, hp, he, temp, hc]


def pair_terms(left, right, d, scale):
    kr = scale * (left[HR] + right[HR])
    vel = [left[HV + k] + right[HV + k] for k in range(3)]
    kp = scale * (left[HP] + right[HP])
    he = left[HE] + right[HE]
    carried = kr * vel[d]
    out = [carried]
    for k in range(3):
        entry = carried * vel[k]
        if k == d:
            entry = entry + kp
        out.append(entry)
    out.append(carried * he + kp * vel[d])
    return out


def face_terms(left, right, d, scale):
    flux = pair_terms(left, right, d, scale)
    speed = jnp.maximum(jnp.abs(left[HV + d]) + left[HC], jnp.abs(right[HV + d]) + right[HC])
    two = (2.0 * scale) * speed
    four = two + two
    out = [flux[0] - two * (right[HR] - left[HR])]
    for k in range(3):
        out.append(flux[k + 1] - four * (right[HR] * right[HV + k] - left[HR] * left[HV + k]))
    out.append(flux[4] - four * (right[HR] * right[HE] - left[HR] * left[HE]))
    return out


def line_inviscid(nodes, f_low, f_high, d):
    scale = 2.4 * JACOBS[d] * STEP_DT
    g = {}
    for i in range(4):
        for j in range(i + 1, 4):
            g[i, j] = pair_terms(nodes[i], nodes[j], d, scale * Q[i][j])
    r0 = [5.0 * (f_low[v] - g[0, 1][v] - g[0, 2][v] - g[0, 3][v]) for v in range(5)]
    r1 = [g[0, 1][v] - g[1, 2][v] - g[1, 3][v] for v in range(5)]
    r2 = [g[0, 2][v] + g[1, 2][v] - g[2, 3][v] for v in range(5)]
    r3 = [5.0 * (g[0, 3][v] + g[1, 3][v] + g[2, 3][v] - f_high[v]) for v in range(5)]
    return r0, r1, r2, r3


def line_derivative(w, low, high, scale):
    c = [[scale * D[i][j] for j in range(4)] for i in range(4)]
    three = 3.0 * scale
    return (
        c[0][1] * w[1] + c[0][2] * w[2] + c[0][3] * w[3] - three * low,
        c[1][0] * w[0] + c[1][2] * w[2] + c[1][3] * w[3],
        c[2][0] * w[0] + c[2][1] * w[1] + c[2][3] * w[3],
        c[3][0] * w[0] + c[3][1] * w[1] + c[3][2] * w[2] + three * high,
    )


def packed(value, at_lane, lane):
    return pltpu.roll(value, lax.rem(at_lane + 128 - lane, 128), 1)


def masks():
    lanes, subs = lane_iota(), sub_iota()
    return lanes, subs, subs < 4, lax.rem(lanes, 2) == 0


def place(columns):
    n = columns[lax.axis_index("span")]
    stream = lax.axis_index("stream")
    return n, stream == 0, stream == lax.axis_size("stream") - 1


W_SCALE = (2.0 * VISC, 2.0 * VISC, 2.0 * VISC, COND)


def readings(prims):
    return [prims[HV], prims[HV + 1], prims[HV + 2], prims[TT]]


def weights_of(lanes, high_end, spans):
    c_of = lanes // 8
    weight = jnp.where((c_of == 0) | (c_of == 3), 1.0 / 6.0, 5.0 / 6.0) / float(4 * spans)
    return jnp.where((lanes < 32) & jnp.logical_not(high_end), weight, 0.0)


def plane_sum(v, n, faces, weight, half):
    total = jnp.where(half < n, faces[0, v] * weight, 0.0)
    return total + jnp.where(2 + half < n, faces[1, v] * weight, 0.0)


def pack_kernel(st_hbm, faces, st, planes, lane_planes, sems):
    lanes, subs, low_half, high_end = masks()
    even_c = lax.rem(lanes // 8, 2) == 0
    loads = [pltpu.make_async_copy(st_hbm.at[s], st.at[s], sems.at[s]) for s in range(4)]
    for load in loads:
        load.start()
    for s in range(4):
        loads[s].wait()

        def per_field(v, carry, s=s):
            for a in range(4):
                acc = jnp.ones((8, 128), F32)
                for k in range(8):
                    target = 16 * (k % 2) + 2 * (k // 2)
                    moved = pltpu.roll(st[s, v, 8 * a + k], target + 1, 1)
                    acc = jnp.where(lanes // 2 == target // 2, moved, acc)
                lane_planes[s, a, v] = acc
            return carry

        lax.fori_loop(0, 5, per_field, 0)
    for q in range(2):
        for a in range(4):
            for v in range(5):
                za, zb = lane_planes[2 * q, a, v], lane_planes[2 * q + 1, a, v]
                even = jnp.where(low_half, za, swap(zb))
                odd = jnp.where(low_half, swap(za), zb)
                planes[q, a, v] = jnp.where(even_c, even, pltpu.roll(odd, 8, 1))
    for q in range(2):
        w = []
        for a in range(4):
            w.append(readings(to_prims([planes[q, a, v] for v in range(5)])))
        for v in range(5):
            faces[q, v] = jnp.where(high_end, planes[q, 3, v], planes[q, 0, v])
        for f in range(4):
            scale = JACOBS[0] * W_SCALE[f]
            near = jnp.where(high_end, w[2][f], w[1][f])
            mid = jnp.where(high_end, w[1][f], w[2][f])
            far = jnp.where(high_end, w[0][f], w[3][f])
            part = (scale * D[3][2]) * near + (scale * D[3][1]) * mid + (scale * D[3][0]) * far
            faces[q, 5 + f] = jnp.where(high_end, part, -part)


def z_pack_kernel(spans, columns, st, own, left, right, opposite, farther, zl, zh, ghosts, sums):
    n, inlet, outlet = place(columns)
    other_n = columns[lax.rem(lax.axis_index("span") + spans // 2, spans)]
    lanes, subs, low_half, high_end = masks()
    half = subs // 4
    used = lanes < 32
    for q in range(2):
        for v in range(9):
            lo, hi = pltpu.roll(left[q, v], 1, 1), pltpu.roll(right[q, v], 127, 1)
            if v < 5:
                lo = jnp.where(inlet, opposite[q, v], lo)
                hi = jnp.where(outlet, own[q, v], hi)
            ghosts[q, v] = jnp.where(used, jnp.where(high_end, hi, lo), 1.0)
    weight = weights_of(lanes, high_end, spans)
    last = n - 1
    last_q, last_half = last // 2, lax.rem(last, 2)
    for v in range(5):
        total = plane_sum(v, n, opposite, weight, half) + plane_sum(v, other_n, farther, weight, half)
        sums[v] = total
        zl[77 + v] = total
        zh[77 + v] = total
        x = ghosts[0, v]
        zl[72 + v] = jnp.where(low_half, x, swap(x))
        x = ghosts[last_q, v]
        take_low = half == last_half
        zh[72 + v] = jnp.where(take_low, x, swap(x))

    dz = [[[JACOBS[2] * W_SCALE[f] * D[i][j] for j in range(4)] for i in range(4)] for f in range(4)]

    def rows(m, carry):
        for side, out in ((0, zl), (1, zh)):
            slot = 0 if side == 0 else last
            parts, states = [], []
            for ab in (m, m + 8):
                u0 = [st[slot, v, 2 * ab] for v in range(5)]
                u1 = [st[slot, v, 2 * ab + 1] for v in range(5)]
                w0, w1 = readings(to_prims(u0)), readings(to_prims(u1))
                part = []
                for f in range(4):
                    c = dz[f]
                    if side == 0:
                        x = jnp.where(low_half, 0.0, c[0][1]) * w0[f]
                        x = x + jnp.where(low_half, c[0][2], c[0][3]) * w1[f]
                    else:
                        x = jnp.where(low_half, c[3][0], c[3][1]) * w0[f]
                        x = x + jnp.where(low_half, c[3][2], 0.0) * w1[f]
                    part.append(x + swap(x))
                parts.append(part)
                states.append(u0 if side == 0 else u1)
            for v in range(5):
                if side == 0:
                    out[8 * v + m] = jnp.where(low_half, states[0][v], swap(states[1][v]))
                else:
                    out[8 * v + m] = jnp.where(low_half, swap(states[0][v]), states[1][v])
            for f in range(4):
                out[8 * (5 + f) + m] = jnp.where(low_half, parts[0][f], parts[1][f])
        return carry

    lax.fori_loop(0, 8, rows, 0)


def small_table(get, lanes, subs):
    b_of = lax.rem(lanes // 2, 4)
    y_of = lax.rem(subs, 4)
    acc = jnp.zeros((8, 128), F32)
    for b in range(4):
        for y in range(4):
            acc = jnp.where((b_of == b) & (y_of == y), get(b, y), acc)
    return acc


def profile_of(t, lanes, high_end):
    t = t + swap(t)
    t = t + pltpu.roll(t, 120, 1)
    t = t + pltpu.roll(t, 112, 1)
    t = jnp.where(lanes < 8, t, pltpu.roll(t, 8, 1))
    t = jnp.where(lanes < 16, t, pltpu.roll(t, 16, 1))
    return jnp.where(high_end, pltpu.roll(t, 127, 1), t)


def packed_derivative(w, step, index, low, high, scale):
    acc = jnp.where(index == 0, (-3.0 * scale) * low, jnp.where(index == 3, (3.0 * scale) * high, 0.0))
    for delta in (-3, -2, -1, 1, 2, 3):
        coefficient = jnp.zeros((8, 128), F32)
        for i in range(4):
            if 0 <= i + delta < 4:
                coefficient = jnp.where(index == i, scale * D[i][i + delta], coefficient)
        acc = acc + coefficient * pltpu.roll(w, (-delta * step) % 128, 1)
    return acc


FIELDS = (HR, HV, HV + 1, HV + 2, HP, HE, HC)
W_FIELDS = (HV, HV + 1, HV + 2, TT)


def direction_pass(d, pairs, n, prim, rate_in, rate, grad, zg, fx, xg):
    lanes, subs, low_half, _ = masks()
    y_of, half = lax.rem(subs, 4), subs // 4
    even_n = lax.rem(n, 2) == 0

    def high_ghost(f, i):
        x = zg[f, i]
        return jnp.where(even_n, x, swap(x))

    scale = 1.2 * JACOBS[d] * STEP_DT

    def per_pair(q, carry):
        slot = 2 * q + half
        before, after = jnp.maximum(q - 1, 0), jnp.minimum(q + 1, 1)

        def line(i, inner):
            base, stride = bases(d, i)
            at = [base + j * stride for j in range(4)]
            nodes = [[prim[q, f, at[j]] for f in range(NPRIM)] for j in range(4)]
            low, high = {}, {}
            if d == 0:
                shift = 127 - lane_of(i)
                for f in FIELDS:
                    low[f] = pltpu.roll(nodes[3][f], 1, 1)
                f_low = face_terms(low, nodes[0], d, scale)
                f_high = []
                for v in range(5):
                    ghost = pltpu.roll(fx[q, v], shift, 1)
                    f_high.append(
                        jnp.where(lanes == 127, ghost, pltpu.roll(f_low[v], 127, 1))
                    )
                    f_low[v] = jnp.where(lanes == 0, ghost, f_low[v])
                for f in W_FIELDS:
                    ghost = pltpu.roll(xg[q, f], shift, 1)
                    x = pltpu.roll(nodes[3][f], 1, 1) if f == TT else low[f]
                    low[f] = jnp.where(lanes == 0, ghost, x)
                    high[f] = jnp.where(lanes == 127, ghost, pltpu.roll(nodes[0][f], 127, 1))
            elif d == 1:
                for f in FIELDS:
                    wall = -nodes[0][f] if f == HV + 1 else nodes[0][f]
                    low[f] = jnp.where(y_of == 0, wall, pltpu.roll(nodes[3][f], 1, 0))
                f_low = face_terms(low, nodes[0], d, scale)
                top = pair_terms(nodes[3], nodes[3], d, scale)
                f_high = [
                    jnp.where(y_of == 3, top[v], pltpu.roll(f_low[v], 7, 0)) for v in range(5)
                ]
                for f in W_FIELDS:
                    if f == TT:
                        low[f] = jnp.where(y_of == 0, nodes[0][f], pltpu.roll(nodes[3][f], 1, 0))
                    elif f != HV + 1:
                        low[f] = jnp.where(y_of == 0, -nodes[0][f], low[f])
                    high[f] = jnp.where(y_of == 3, nodes[3][f], pltpu.roll(nodes[0][f], 7, 0))
            else:
                for f in range(NPRIM):
                    prev, nxt = prim[before, f, at[3]], prim[after, f, at[0]]
                    x = swap(jnp.where(low_half, nodes[3][f], prev))
                    low[f] = jnp.where(slot == 0, zg[f, i], x)
                    x = swap(jnp.where(low_half, nxt, nodes[0][f]))
                    high[f] = jnp.where(slot == n - 1, high_ghost(f, i), x)
                f_low = face_terms(low, nodes[0], d, scale)
                f_high = face_terms(nodes[3], high, d, scale)
            change = line_inviscid(nodes, f_low, f_high, d)
            for j in range(4):
                for v in range(5):
                    if rate_in is None:
                        rate[q, v, at[j]] = change[j][v]
                    else:
                        rate[q, v, at[j]] = rate_in[q, v, at[j]] + change[j][v]
            for k, f in enumerate(W_FIELDS):
                lifted = line_derivative(
                    [nodes[j][f] for j in range(4)], low[f], high[f], JACOBS[d] * W_SCALE[k]
                )
                for j in range(4):
                    grad[q, k, at[j]] = lifted[j]
            return inner

        if d == 0:
            for i in range(16):
                line(i, 0)
            return carry
        return lax.fori_loop(0, 16, line, carry, unroll=2)

    lax.fori_loop(0, pairs, per_pair, 0)


def y_kernel(columns, st, sums, prim, rate, grad, passed):
    n, _, _ = place(columns)
    pairs = (n + 1) // 2
    _, _, low_half, _ = masks()

    def prims_of(q, carry):
        def nodes(kk, inner):
            first, second = [], []
            for v in range(5):
                a, b = st[2 * q, v, kk], st[2 * q + 1, v, kk]
                first.append(jnp.where(low_half, a, swap(b)))
                second.append(jnp.where(low_half, swap(a), b))
            for f, x in enumerate(to_prims(first)):
                prim[q, f, 2 * kk] = x
            for f, x in enumerate(to_prims(second)):
                prim[q, f, 2 * kk + 1] = x
            return inner

        return lax.fori_loop(0, 32, nodes, carry, unroll=2)

    lax.fori_loop(0, pairs, prims_of, 0)
    direction_pass(1, pairs, n, prim, None, rate, grad, None, None, None)
    passed[...] = sums[...]


def sum_kernel(sums, zfl, zfr, after, out):
    for v in range(5):
        out[v] = (sums[v] + after[v]) + (zfl[77 + v] + zfr[77 + v])


def z_kernel(columns, prim, rate_in, zfl, zfr, rate, grad, zg, part):
    n, _, _ = place(columns)
    pairs = (n + 1) // 2
    _, _, low_half, _ = masks()

    def z_ghost(m, carry):
        first, second = [], []
        for v in range(9):
            a, b = zfl[8 * v + m], zfr[8 * v + m]
            first.append(jnp.where(low_half, a, swap(b)))
            second.append(jnp.where(low_half, swap(a), b))
        for ab, u in ((m, first), (m + 8, second)):
            for f, x in enumerate(to_prims(u[:5])):
                zg[f, ab] = x
            for f in range(4):
                part[f, ab] = u[5 + f]
        return carry

    lax.fori_loop(0, 8, z_ghost, 0, unroll=2)
    direction_pass(2, pairs, n, prim, rate_in, rate, grad, zg, None, None)


GFIELDS = ((0, 1, 2, 6), (1, 3, 4, 7), (2, 4, 5, 8))


def section_kernel(
    columns, target, gain, st, own, opposite, ghosts, zfl, zfr, w4, w4_far, prim, rate_in, grad_y, grad_z, zg, part,
    out, xg, gx, fx, gz, gzh, grad_x, rate, gflux, rec, corner, dpart,
):
    n, inlet, outlet = place(columns)
    pairs = (n + 1) // 2
    lanes, subs, low_half, high_end = masks()
    y_of = lax.rem(subs, 4)
    half = subs // 4
    used = lanes < 32
    last_q = (n - 1) // 2
    even_n = lax.rem(n, 2) == 0

    gains = small_table(lambda b, y: gain[b, y], lanes, subs)
    raw = [[], []]
    corners = [[], []]
    for v in range(5):
        profile = profile_of(w4[v] + w4_far[v], lanes, high_end)
        wanted = small_table(lambda b, y, v=v: target[b, y, v], lanes, subs)
        for q in range(2):
            rec[q, v] = wanted + gains * (opposite[q, v] - profile)
            x = ghosts[q, v]
            y = jnp.where(inlet, wanted + gains * (x - profile), x)
            raw[q].append(jnp.where(used, jnp.where(high_end, x, y), 1.0))
        for side, src in enumerate((zfl, zfr)):
            x = src[72 + v]
            y = jnp.where(inlet, wanted + gains * (x - profile), x)
            x = jnp.where(high_end, x, y)
            corners[side].append(jnp.where(used, x, 1.0))
    for q in range(2):
        for f, x in enumerate(to_prims(raw[q])):
            xg[q, f] = x
    corner_w = [readings(to_prims(corners[side])) for side in range(2)]
    for f in range(4):
        corner[f] = jnp.where(low_half, pltpu.roll(corner_w[0][f], 104, 1), corner_w[1][f])

    own_p = [to_prims([jnp.where(used, own[q, v], 1.0) for v in range(5)]) for q in range(2)]
    b_of, c_of = lax.rem(lanes // 2, 4), lanes // 8
    ghost_w = [[xg[q, HV], xg[q, HV + 1], xg[q, HV + 2], xg[q, TT]] for q in range(2)]
    for q in range(2):
        w = ghost_w[q]
        qx = []
        for f in range(4):
            o = (3.0 * JACOBS[0] * W_SCALE[f]) * readings(own_p[q])[f]
            qx.append(ghosts[q, 5 + f] + jnp.where(high_end, -o, o))
        dy = []
        for f in range(2):
            low = pltpu.roll(pltpu.roll(w[f], 122, 1), 1, 0)
            low = jnp.where(y_of == 0, -w[f], low)
            high = pltpu.roll(pltpu.roll(w[f], 6, 1), 7, 0)
            high = jnp.where(y_of == 3, w[f], high)
            dy.append(packed_derivative(w[f], 2, b_of, low, high, JACOBS[1] * W_SCALE[f]))
        dz = []
        slot = 2 * q + half
        for f in (0, 2):
            low = swap(jnp.where(low_half, w[f], ghost_w[max(q - 1, 0)][f]))
            low = pltpu.roll(jnp.where(slot == 0, corner_w[0][f], low), 104, 1)
            high = swap(jnp.where(low_half, ghost_w[min(q + 1, 1)][f], w[f]))
            high = pltpu.roll(jnp.where(slot == n - 1, corner_w[1][f], high), 24, 1)
            dz.append(packed_derivative(w[f], 8, c_of, low, high, JACOBS[2] * W_SCALE[f]))
        spread = (2.0 / 3.0) * (qx[0] + dy[1] + dz[1])
        t = [(qx[0] + qx[0]) - spread, qx[1] + dy[0], qx[2] + dz[0]]
        h = w[0] * t[0] + w[1] * t[1] + w[2] * t[2]
        for f, x in enumerate((*t, (h + h) + qx[3])):
            gx[q, f] = x
        for k in range(3):
            x = xg[q, HV + k] - own_p[q][HV + k]
            gx[q, 4 + k] = x + x
        ghost = [xg[q, f] for f in range(NPRIM)]
        first = [jnp.where(high_end, own_p[q][f], ghost[f]) for f in range(NPRIM)]
        second = [jnp.where(high_end, ghost[f], own_p[q][f]) for f in range(NPRIM)]
        for v, x in enumerate(face_terms(first, second, 0, 1.2 * JACOBS[0] * STEP_DT)):
            step = (0.2 * STEP_DT * RELAX) * (rec[q, v] - own[q, v])
            fx[q, v] = x + jnp.where(high_end, 0.0, step)

    def ghost_lines(i, carry):
        at = [4 * j + i for j in range(4)]
        for k, f in enumerate((0, 2)):
            w = [zg[HV + f, at[j]] for j in range(4)]
            ghost = pltpu.roll(corner[f], 127 - 2 * i, 1)
            low = jnp.where(lanes == 0, ghost, pltpu.roll(w[3], 1, 1))
            high = jnp.where(lanes == 127, ghost, pltpu.roll(w[0], 127, 1))
            for j, x in enumerate(line_derivative(w, low, high, JACOBS[0] * W_SCALE[f])):
                dpart[k, at[j]] = x
        at = [4 * i + j for j in range(4)]
        for k, f in enumerate((1, 2)):
            w = [zg[HV + f, at[j]] for j in range(4)]
            low = jnp.where(y_of == 0, -w[0], pltpu.roll(w[3], 1, 0))
            high = jnp.where(y_of == 3, w[3], pltpu.roll(w[0], 7, 0))
            for j, x in enumerate(line_derivative(w, low, high, JACOBS[1] * W_SCALE[f])):
                dpart[2 + k, at[j]] = x
        return carry

    for i in range(4):
        ghost_lines(i, 0)

    def ghost_flux(ab, carry):
        qz = []
        for f in range(4):
            src = HV + f if f < 3 else TT
            x = prim[last_q, src, 4 * ab + 3]
            o = jnp.where(low_half, prim[0, src, 4 * ab], jnp.where(even_n, x, swap(x)))
            o = (3.0 * JACOBS[2] * W_SCALE[f]) * o
            qz.append(part[f, ab] + jnp.where(low_half, o, -o))
        spread = (2.0 / 3.0) * (dpart[0, ab] + dpart[2, ab] + qz[2])
        t = [qz[0] + dpart[1, ab], qz[1] + dpart[3, ab], (qz[2] + qz[2]) - spread]
        h = zg[HV, ab] * t[0] + zg[HV + 1, ab] * t[1] + zg[HV + 2, ab] * t[2]
        for f, x in enumerate((*t, (h + h) + qz[3])):
            gz[f, ab] = x
            gzh[f, ab] = jnp.where(even_n, x, swap(x))
        return carry

    lax.fori_loop(0, 16, ghost_flux, 0, unroll=4)

    direction_pass(0, pairs, n, prim, rate_in, rate, grad_x, None, fx, xg)

    def fluxes(q, carry):
        def node(m, inner):
            e = [grad[q, k, m] for grad in (grad_x, grad_y, grad_z) for k in range(4)]
            hv = [prim[q, HV + k, m] for k in range(3)]
            spread = (2.0 / 3.0) * (e[0] + e[5] + e[10])
            t = {}
            for i in range(3):
                t[i, i] = (e[5 * i] + e[5 * i]) - spread
                for j in range(i + 1, 3):
                    t[i, j] = t[j, i] = e[4 * i + j] + e[4 * j + i]
            for index, key in enumerate(((0, 0), (0, 1), (0, 2), (1, 1), (1, 2), (2, 2))):
                gflux[q, index, m] = t[key]
            for i in range(3):
                h = hv[0] * t[i, 0] + hv[1] * t[i, 1] + hv[2] * t[i, 2]
                gflux[q, 6 + i, m] = (h + h) + e[4 * i + 3]
            return inner

        return lax.fori_loop(0, 64, node, carry, unroll=4)

    lax.fori_loop(0, pairs, fluxes, 0)

    def divergence(d):
        def per_pair(q, carry):
            slot = 2 * q + half
            before, after = jnp.maximum(q - 1, 0), jnp.minimum(q + 1, 1)
            second = 2 * q + 1 < n

            def line(i, inner):
                base, stride = bases(d, i)
                at = [base + j * stride for j in range(4)]
                g = [[gflux[q, f, at[j]] for f in GFIELDS[d]] for j in range(4)]
                low, high = [], []
                if d == 0:
                    shift = 127 - lane_of(i)
                    inner_low = list(g[0])
                    for k in range(3):
                        inner_low[3] = inner_low[3] + pltpu.roll(gx[q, 4 + k], shift, 1) * g[0][k]
                    for f in range(4):
                        ghost = pltpu.roll(gx[q, f], shift, 1)
                        x = jnp.where(inlet, inner_low[f], ghost)
                        low.append(jnp.where(lanes == 0, x, pltpu.roll(g[3][f], 1, 1)))
                        x = jnp.where(outlet, g[3][f], ghost)
                        high.append(jnp.where(lanes == 127, x, pltpu.roll(g[0][f], 127, 1)))
                elif d == 1:
                    for f in range(4):
                        low.append(jnp.where(y_of == 0, g[0][f], pltpu.roll(g[3][f], 1, 0)))
                        high.append(jnp.where(y_of == 3, g[3][f], pltpu.roll(g[0][f], 7, 0)))
                else:
                    for f in range(4):
                        src = GFIELDS[d][f]
                        prev, nxt = gflux[before, src, at[3]], gflux[after, src, at[0]]
                        x = swap(jnp.where(low_half, g[3][f], prev))
                        low.append(jnp.where(slot == 0, gz[f, i], x))
                        x = swap(jnp.where(low_half, nxt, g[0][f]))
                        high.append(jnp.where(slot == n - 1, gzh[f, i], x))
                total = [[rate[q, 0, at[j]] for j in range(4)]] if d == 2 else []
                for f in range(4):
                    change = line_derivative(
                        [g[j][f] for j in range(4)], low[f], high[f], JACOBS[d] * STEP_DT
                    )
                    if d == 2:
                        total.append([rate[q, f + 1, at[j]] + change[j] for j in range(4)])
                    else:
                        for j in range(4):
                            rate[q, f + 1, at[j]] = rate[q, f + 1, at[j]] + change[j]
                if d == 2:
                    for v in range(5):
                        for m in range(2):
                            x, y = total[v][2 * m], total[v][2 * m + 1]
                            kk = 2 * i + m
                            out[2 * q, v, kk] = st[2 * q, v, kk] + jnp.where(low_half, x, swap(y))
                            b = st[2 * q + 1, v, kk]
                            z = b + jnp.where(low_half, swap(x), y)
                            out[2 * q + 1, v, kk] = jnp.where(second, z, b)
                return inner

            if d == 0:
                for i in range(16):
                    line(i, 0)
                return carry
            return lax.fori_loop(0, 16, line, carry, unroll=2)

        lax.fori_loop(0, pairs, per_pair, 0)

    for d in range(3):
        divergence(d)

    @pl.when(pairs == 1)
    def _():
        out[2] = st[2]
        out[3] = st[3]


def shape(*dims):
    return jax.ShapeDtypeStruct(dims, F32)


def vspec():
    return pl.BlockSpec(memory_space=pltpu.VMEM)


def sspec():
    return pl.BlockSpec(memory_space=pltpu.SMEM)


def params(mib):
    return pltpu.CompilerParams(vmem_limit_bytes=mib << 20)


def shifted(array, axis, by):
    count = lax.axis_size(axis)
    return lax.ppermute(array, axis, [(i, (i + by) % count) for i in range(count)])


def opposite_shifted(array, by):
    streams, spans = lax.axis_size("stream"), lax.axis_size("span")
    pairs = []
    for i in range(streams):
        for p in range(spans):
            to = (i + streams // 2) % streams * spans + (p - by) % spans
            pairs.append((i * spans + p, to))
    return lax.ppermute(array, ("stream", "span"), pairs)


def cost(mib):
    return pl.CostEstimate(flops=mib << 22, transcendentals=0, bytes_accessed=mib << 20)


def vmem(*dims):
    return pltpu.VMEM(dims, F32)


def on_device(state, columns, target_profile, fluct_gain):
    st = state.reshape(4, 5, 32, 8, 128)
    streams, spans = lax.axis_size("stream"), lax.axis_size("span")
    own = pl.pallas_call(
        pack_kernel,
        out_shape=shape(2, 9, 8, 128),
        in_specs=[pl.BlockSpec(memory_space=pltpu.MemorySpace.HBM)],
        out_specs=vspec(),
        scratch_shapes=[
            vmem(4, 5, 32, 8, 128),
            vmem(2, 4, 5, 8, 128),
            vmem(4, 4, 5, 8, 128),
            pltpu.SemaphoreType.DMA((4,)),
        ],
        compiler_params=params(62),
        name="x_faces",
    )(st)
    left = shifted(own, "stream", 1)
    right = shifted(own, "stream", -1)
    opposite = shifted(own, "stream", streams // 2)
    farther = opposite_shifted(own, spans // 2)
    zl, zh, ghosts, sums = pl.pallas_call(
        functools.partial(z_pack_kernel, spans),
        out_shape=(shape(82, 8, 128), shape(82, 8, 128), shape(2, 9, 8, 128), shape(5, 8, 128)),
        in_specs=[sspec()] + [vspec()] * 6,
        out_specs=(vspec(),) * 4,
        compiler_params=params(4),
        name="z_faces",
    )(columns, st, own, left, right, opposite, farther)
    zfl = shifted(zh, "span", 1)
    zfr = shifted(zl, "span", -1)
    after = shifted(sums, "span", -2)
    prim, rate, grad_y, sums = pl.pallas_call(
        y_kernel,
        out_shape=(
            shape(2, NPRIM, 64, 8, 128),
            shape(2, 5, 64, 8, 128),
            shape(2, 4, 64, 8, 128),
            shape(5, 8, 128),
        ),
        in_specs=[sspec(), vspec(), vspec()],
        out_specs=(vspec(),) * 4,
        compiler_params=params(4),
        cost_estimate=cost(16),
        name="y_direction",
    )(columns, st, sums)
    w4 = pl.pallas_call(
        sum_kernel,
        out_shape=shape(5, 8, 128),
        in_specs=[vspec()] * 4,
        out_specs=vspec(),
        compiler_params=params(2),
        name="sums",
    )(sums, zfl, zfr, after)
    w4_far = shifted(w4, "span", spans // 4)
    rate, grad_z, zg, part = pl.pallas_call(
        z_kernel,
        out_shape=(
            shape(2, 5, 64, 8, 128),
            shape(2, 4, 64, 8, 128),
            shape(NPRIM, 16, 8, 128),
            shape(4, 16, 8, 128),
        ),
        in_specs=[sspec()] + [vspec()] * 4,
        out_specs=(vspec(),) * 4,
        input_output_aliases={2: 0},
        compiler_params=params(4),
        cost_estimate=cost(16),
        name="z_direction",
    )(columns, prim, rate, zfl, zfr)
    out = pl.pallas_call(
        section_kernel,
        out_shape=shape(4, 5, 32, 8, 128),
        in_specs=[sspec()] * 3 + [vspec()] * 14,
        out_specs=vspec(),
        scratch_shapes=[
            vmem(2, NPRIM, 8, 128),
            vmem(2, 7, 8, 128),
            vmem(2, 5, 8, 128),
            vmem(4, 16, 8, 128),
            vmem(4, 16, 8, 128),
            vmem(2, 4, 64, 8, 128),
            vmem(2, 5, 64, 8, 128),
            vmem(2, 9, 64, 8, 128),
            vmem(2, 5, 8, 128),
            vmem(4, 8, 128),
            vmem(4, 16, 8, 128),
        ],
        compiler_params=params(14),
        name="section",
    )(
        columns, target_profile.transpose(1, 2, 0), fluct_gain, st, own, opposite, ghosts, zfl, zfr, w4, w4_far,
        prim, rate, grad_y, grad_z, zg, part,
    )
    return out.reshape(state.shape)


def solution(mesh):
    placed = (P("span", None, None, None, "stream"), P(), P(), P())
    return jax.shard_map(
        on_device,
        mesh=mesh,
        in_specs=placed,
        out_specs=P("span", None, None, None, "stream"),
        check_vma=False,
    )
```
